256 devices in a mesh: cube: 16 (over z, x_hi), row: 4 (over x_lo, core), col: 4 (over y).
Axes of the slice: x: 4 (x_hi: 2, x_lo: 2; x = x_hi * 2 + x_lo), y: 4, z: 8, core: 2. Of those that a mesh axis runs over, the one named last changes fastest.
Arguments:
- diag_block: float32 [16, 512, 512], P('cube'), as said below
- panel: float32 [16, 8192, 512], P('cube', ('row', 'col')), may hold values from -2.4 to 2.4
- trailing: float32 [16, 2048, 8192], P('cube', 'col', 'row'), may hold values from -6 to 6
- parent_front: float32 [16, 512, 8192], P('cube', 'col', 'row'), may hold values from -6 to 6
- front_order: int32 [16], P('cube'), may hold values from 4096 to 8192, as said below
- dest_group: int32 [16, 4, 4, 64, 1], P(None, 'col', 'row'), may hold values from 0 to 15; in each aligned block of 64 rows (0 to 63, 64 to 127, ..., all dimensions but the last counted through in order) at most 8 rows name the same one
- parent_block: int32 [16, 4, 4, 64, 1], P(None, 'col', 'row'), may hold values from 0 to 15
Outputs:
- assembled: float32 [16, 512, 8192], P('cube', 'col', 'row')
The draws below stay inside these ranges and needn't reach their ends.
Inputs may be any that keep to these rules, and one draw needn't show every extreme that they name: `front_order`: a multiple of 128; each group's update matrix is zero in the columns at or beyond it. `dest_group`: at most 8 of the 64 blocks of one device and group go to one group. `diag_block`: symmetric positive definite.
All inputs are finite; a program needn't handle non-finite values.
Results may differ from the reference program's by a relative error of at most 0.0003.
Values sent between devices are 32-bit elements; how exact they have to be, the bound alone decides.
A program may use at most 128 MiB of HBM per device.

```python
import math
import jax
import jax.numpy as jnp
import numpy as np
from jax import lax

BS = 128
P_SIZE = 512
M = 8192
SLAB = 2048
PARENT = 512
BLK_DEV = 64
PB_DEV = 16
CAP = 8
N_CUBE = 16
N_ROW = 4
N_COL = 4


def draw_diag_block(key, part):
    key_dense = jax.random.fold_in(key, 11)
    key_near = jax.random.fold_in(key, 12)
    key_third = jax.random.fold_in(key, 13)
    key_main = jax.random.fold_in(key, 14)
    dense = jax.random.uniform(key_dense, (N_CUBE, P_SIZE, P_SIZE), jnp.float32, -0.5 / P_SIZE, 0.5 / P_SIZE)
    near = jax.random.uniform(key_near, (N_CUBE, P_SIZE, P_SIZE), jnp.float32, -1.0, -0.3)
    third = jax.random.uniform(key_third, (N_CUBE, P_SIZE, P_SIZE), jnp.float32, -0.5, 0.5)
    diagonal = jax.random.uniform(key_main, (N_CUBE, P_SIZE), jnp.float32, 3.6, 5.0)
    row_ids = jnp.arange(P_SIZE, dtype=jnp.int32)[:, None]
    col_ids = jnp.arange(P_SIZE, dtype=jnp.int32)[None, :]
    distance = jnp.abs(row_ids - col_ids)[None, :, :]
    values = jnp.where(distance == 1, near, jnp.where(distance == 3, third, dense))
    symmetric = (values + jnp.swapaxes(values, 1, 2)) * 0.5
    return jnp.where(distance == 0, diagonal[:, :, None], symmetric)


def draw_front_order(key, part):
    key_pick = jax.random.fold_in(key, 7)
    key_levels = jax.random.fold_in(key, 8)
    levels = jax.random.randint(key_levels, (N_CUBE,), M // (2 * BS), M // BS + 1)
    widest = jax.random.randint(key_pick, (), 0, N_CUBE)
    levels = jnp.where(jnp.arange(N_CUBE) == widest, M // BS, levels)
    return (levels * BS).astype(jnp.int32)


def plant(values, stream_key, smallest, top_value):
    spot = [jax.random.randint(jax.random.fold_in(stream_key, axis), (), 0, length) for axis, length in enumerate(values.shape)]
    widest = values.shape.index(max(values.shape))
    next_to = spot[:widest] + [(spot[widest] + 1) % values.shape[widest]] + spot[widest + 1:]
    return values.at[tuple(spot)].set(smallest).at[tuple(next_to)].set(top_value)


def block_levels(key, dims, split, smallest, high):
    gain = 1.0
    for axis_at, blocks in split:
        heights = jax.random.uniform(jax.random.fold_in(jax.random.fold_in(key, 6), axis_at), (blocks,), jnp.float32, smallest / len(split), high / len(split))
        gain = gain * jnp.repeat(jnp.exp(heights), dims[axis_at] // blocks).reshape((-1,) + (1,) * (len(dims) - 1 - axis_at))
    return gain


def assign_block(own_key, own, number, rows, count, top, reach, skew):
    ranking = jax.random.permutation(own_key, count)
    packed, usual = load_shares(count, rows * top, reach, skew, True), load_shares(count, rows * top, reach, skew, False)
    places = jnp.arange(count)

    def named(sizes, rotation):
        used = int((sizes > 0).sum())
        fixed = max(1, used // 4)
        shifted = fixed + (places - fixed + rotation * (used - fixed)) % max(1, count - fixed)
        return jnp.zeros((count,), jnp.int32).at[ranking[jnp.where(places < fixed, places, shifted)]].set(jnp.asarray(sizes, jnp.int32))

    sizes = jnp.where(number % 4 == 0, named(packed, number // 4), named(usual, number - number // 4 - 1))
    mixed = jax.random.permutation(jax.random.fold_in(own, 3), count)
    source_of, taker = mixed[0:count // 2 * 2:2], mixed[1:count // 2 * 2:2]
    margin = jnp.minimum(sizes[source_of] - 1, reach - sizes[taker]) // 2
    margin = jnp.where((source_of == ranking[0]) | (taker == ranking[0]) | (sizes[taker] == 0), 0, jnp.maximum(margin, 0))
    shifted = jax.random.randint(jax.random.fold_in(own, 4), (count // 2,), 0, 1 << 20) % (margin + 1)
    sizes = sizes.at[source_of].add(-shifted).at[taker].add(shifted)
    items = jnp.searchsorted(jnp.cumsum(sizes), jnp.arange(rows * top), side="right").astype(jnp.int32)
    grid = items.reshape(top, rows).T
    grid = grid[jax.random.permutation(jax.random.fold_in(own, 1), rows)]
    rotation = jax.random.randint(jax.random.fold_in(own, 2), (rows, 1), 0, top)
    return jnp.take_along_axis(grid, (jnp.arange(top)[None, :] + rotation) % top, axis=1)


def load_shares(amount, total, reach, slope, full):
    weights = [(1 << 20) // math.isqrt(rank ** slope) + 1 for rank in range(1, amount + 1)]
    largest = reach if full else min(reach, max(-(-total // amount), total * weights[0] // sum(weights)))
    least = 1 if total - largest >= amount - 1 else 0
    holding, spare = [largest] + [least] * (amount - 1), total - largest - least * (amount - 1)
    while spare > 0:
        movable = [i for i in range(1, amount) if holding[i] < largest] or [i for i in range(1, amount) if holding[i] < reach]
        mass, left = sum([weights[i] for i in movable]), spare
        for i in movable:
            more = min(reach - holding[i], max(1, left * weights[i] // mass), spare)
            holding[i] = holding[i] + more
            spare = spare - more
    return np.array(holding)


def normal_values(rng, extent, width, bound, pieces=(), kind=jnp.bfloat16):
    entries = width * jax.random.normal(rng, extent, jnp.float32)
    if pieces:
        entries = entries * block_levels(rng, extent, pieces, -0.22, 0.18)
    return jnp.clip(entries, -bound, bound).astype(kind)


def setup_inputs(seed: int = 0) -> dict:
    arg_keys = jax.random.split(jax.random.key(seed), 8)
    diag_block = draw_diag_block(jax.random.fold_in(arg_keys[7], 71), 0)
    panel = normal_values(arg_keys[1], (N_CUBE, M, P_SIZE), 0.3, 2.4, ((0, 16), (1, 16)), jnp.float32)
    trailing = normal_values(arg_keys[2], (N_CUBE, SLAB, M), 1.0, 6.0, ((0, 16), (1, 4), (2, 4)), jnp.float32)
    parent_front = normal_values(arg_keys[3], (N_CUBE, PARENT, M), 1.0, 6.0, ((0, 16), (1, 4), (2, 4)), jnp.float32)
    front_order = draw_front_order(jax.random.fold_in(arg_keys[7], 71), 0)
    dest_group_keys = jax.random.split(jax.random.fold_in(arg_keys[5], 1), N_CUBE * N_COL * N_ROW * BLK_DEV // BLK_DEV)
    dest_group_turns = jax.random.permutation(jax.random.fold_in(arg_keys[5], 3), N_CUBE * N_COL * N_ROW * BLK_DEV // BLK_DEV)
    dest_group = jax.vmap(lambda own, number: assign_block(jax.random.fold_in(arg_keys[5], 2), own, number, BLK_DEV, N_CUBE, 1, CAP, 1))(dest_group_keys, dest_group_turns).reshape((N_CUBE, N_COL, N_ROW, BLK_DEV, 1))
    parent_block = plant(jax.random.randint(arg_keys[6], (N_CUBE, N_COL, N_ROW, BLK_DEV, 1), 0, PB_DEV), jax.random.fold_in(arg_keys[6], 1), 0, PB_DEV - 1).astype(jnp.int32)
    return dict(diag_block=diag_block, panel=panel, trailing=trailing, parent_front=parent_front, front_order=front_order, dest_group=dest_group, parent_block=parent_block)


def to_blocks(matrix, device_rows):
    cols_dev = M // N_ROW
    tiles = matrix.reshape(N_COL, device_rows // BS, BS, N_ROW, cols_dev // BS, BS)
    tiles = tiles.transpose(0, 3, 1, 4, 2, 5)
    return tiles.reshape(N_COL, N_ROW, device_rows // BS * (cols_dev // BS), BS * BS)

def from_blocks(blocks, device_rows):
    cols_dev = M // N_ROW
    tiles = blocks.reshape(N_COL, N_ROW, device_rows // BS, cols_dev // BS, BS, BS)
    tiles = tiles.transpose(0, 2, 4, 1, 3, 5)
    return tiles.reshape(N_COL * device_rows, M)

def reference(diag_block, panel, trailing, parent_front, front_order, dest_group, parent_block):
    device_rows = M // (N_ROW * N_COL)
    parent_rows = M // N_ROW // 4 // N_COL
    col_ids = jnp.arange(N_COL, dtype=jnp.int32)[:, None, None]
    row_ids = jnp.arange(N_ROW, dtype=jnp.int32)[None, :, None]

    def source(totals, group_id):
        chol_diag = jnp.linalg.cholesky(diag_block[group_id])
        panel_factor = lax.linalg.triangular_solve(chol_diag, panel[group_id], left_side=False, lower=True, transpose_a=True)
        product = jnp.dot(panel_factor[:M // N_ROW], panel_factor.T, precision=lax.Precision.HIGHEST)
        update = trailing[group_id] - product
        live = jnp.arange(M, dtype=jnp.int32)[None, :] < front_order[group_id]
        update = jnp.where(live, update, jnp.float32(0.0))
        blocks = to_blocks(update, device_rows)
        targets = dest_group[group_id, :, :, :, 0]
        parent_ids = parent_block[group_id, :, :, :, 0]
        totals = totals.at[targets, col_ids, row_ids, parent_ids].add(blocks)
        return (totals, None)
    initial = jax.vmap(lambda matrix: to_blocks(matrix, parent_rows))(parent_front)
    totals, _ = lax.scan(source, initial, jnp.arange(N_CUBE, dtype=jnp.int32))
    return jax.vmap(lambda blocks: from_blocks(blocks, parent_rows))(totals)
```

```python
import jax
import jax.numpy as jnp
from jax import lax
from jax.sharding import PartitionSpec as P

BS = 128


def spread(value, axis, root):
    mine = lax.axis_index(axis) == root
    return lax.psum(jnp.where(mine, value, jnp.zeros_like(value)), axis)


def shards(diag_block, panel, trailing, parent_front, front_order, dest_group, parent_block):
    precise_mode = lax.Precision.HIGHEST
    slab_rows = spread(panel[0], "row", 0)
    col_rows = lax.all_gather(panel[0], "col", axis=0, tiled=True)
    chol_diag = jnp.linalg.cholesky(diag_block[0])
    order = chol_diag.shape[0]
    chol_inv = lax.linalg.triangular_solve(
        chol_diag, jnp.eye(order, dtype=chol_diag.dtype), left_side=True, lower=True
    )
    contract_t = (((1,), (1,)), ((), ()))
    slab_factor = lax.dot_general(slab_rows, chol_inv, contract_t, precision=precise_mode)
    col_factor = lax.dot_general(col_rows, chol_inv, contract_t, precision=precise_mode)
    product = lax.dot_general(slab_factor, col_factor, contract_t, precision=precise_mode)
    device_rows = trailing.shape[1]
    cols_dev = trailing.shape[2]
    column_ids = lax.axis_index("row") * cols_dev + jnp.arange(cols_dev, dtype=jnp.int32)
    update = jnp.where(
        column_ids[None, :] < front_order[0], trailing[0] - product, jnp.float32(0.0)
    )
    block_rows = device_rows // BS
    block_cols = cols_dev // BS
    blocks = (
        update.reshape(block_rows, BS, block_cols, BS)
        .transpose(0, 2, 1, 3)
        .reshape(block_rows * block_cols, BS * BS)
    )
    nblocks = block_rows * block_cols
    groups = lax.axis_size("cube")
    own_group = lax.axis_index("cube")
    dest_all = dest_group[:, 0, 0, :, 0]
    parent_all = parent_block[:, 0, 0, :, 0]
    dest_mine = lax.dynamic_index_in_dim(dest_all, own_group, 0, keepdims=False)
    parent_rows = parent_front.shape[1]
    parent_brows = parent_rows // BS
    nparent = parent_brows * block_cols
    capacity = 2 * nblocks // groups
    hit_table = (dest_mine[:, None] == jnp.arange(groups, dtype=jnp.int32)[None, :]).astype(
        jnp.int32
    )
    before = jnp.cumsum(hit_table, axis=0) - hit_table
    slot_ids = jnp.sum(before * hit_table, axis=1)
    position = dest_mine * capacity + slot_ids
    picker = (position[None, :] == jnp.arange(groups * capacity, dtype=jnp.int32)[:, None]).astype(
        jnp.float32
    )
    outgoing = jnp.dot(picker, blocks, precision=precise_mode).reshape(groups, capacity, BS * BS)
    incoming = lax.all_to_all(outgoing, "cube", split_axis=0, concat_axis=0, tiled=True)
    arriving = (dest_all == own_group).astype(jnp.int32)
    rank_ids = jnp.cumsum(arriving, axis=1) - arriving
    in_slot = (
        arriving[:, :, None]
        * (rank_ids[:, :, None] == jnp.arange(capacity, dtype=jnp.int32)[None, None, :])
    ).astype(jnp.float32)
    to_parent = (
        parent_all[:, :, None] == jnp.arange(nparent, dtype=jnp.int32)[None, None, :]
    ).astype(jnp.float32)
    weight = jnp.einsum("sbk,sbp->psk", in_slot, to_parent, precision=precise_mode)
    assembled = jnp.dot(
        weight.reshape(nparent, groups * capacity),
        incoming.reshape(groups * capacity, BS * BS),
        precision=precise_mode,
    )
    assembled = (
        assembled.reshape(parent_brows, block_cols, BS, BS)
        .transpose(0, 2, 1, 3)
        .reshape(parent_rows, cols_dev)
    )
    return (parent_front[0] + assembled)[None]


def solution(mesh):
    placed = (
        P("cube", None, None),
        P("cube", ("row", "col"), None),
        P("cube", "col", "row"),
        P("cube", "col", "row"),
        P("cube"),
        P(None, "col", "row", None, None),
        P(None, "col", "row", None, None),
    )
    return jax.shard_map(
        shards, mesh=mesh, in_specs=placed, out_specs=P("cube", "col", "row"), check_vma=False
    )
```

```python
import jax
import jax.numpy as jnp
from jax import lax
from jax.sharding import PartitionSpec as P

BS = 128


def spread(value, axis, root):
    mine = lax.axis_index(axis) == root
    return lax.psum(jnp.where(mine, value, jnp.zeros_like(value)), axis)


def invert_lower(chol, precision):
    order = chol.shape[0]
    nb = order // BS
    diag = jnp.stack([chol[k * BS:(k + 1) * BS, k * BS:(k + 1) * BS] for k in range(nb)])
    eye = jnp.broadcast_to(jnp.eye(BS, dtype=chol.dtype), diag.shape)
    diag_inv = lax.linalg.triangular_solve(diag, eye, left_side=True, lower=True)
    rows = [jnp.concatenate([diag_inv[0], jnp.zeros((BS, order - BS), chol.dtype)], axis=1)]
    for i in range(1, nb):
        done = jnp.concatenate([r[:, :i * BS] for r in rows], axis=0)
        mixed = jnp.dot(chol[i * BS:(i + 1) * BS, :i * BS], done, precision=precision)
        left = -jnp.dot(diag_inv[i], mixed, precision=precision)
        pieces = [left, diag_inv[i]]
        if i < nb - 1:
            pieces.append(jnp.zeros((BS, order - (i + 1) * BS), chol.dtype))
        rows.append(jnp.concatenate(pieces, axis=1))
    return jnp.concatenate(rows, axis=0)


def shards(diag_block, panel, trailing, parent_front, front_order, dest_group, parent_block):
    precise_mode = lax.Precision.HIGHEST
    slab_rows = spread(panel[0], "row", 0)
    col_rows = lax.all_gather(panel[0], "col", axis=0, tiled=True)
    chol_diag = jnp.linalg.cholesky(diag_block[0])
    order = chol_diag.shape[0]
    chol_inv = invert_lower(chol_diag, precise_mode)
    contract_t = (((1,), (1,)), ((), ()))
    slab_factor = lax.dot_general(slab_rows, chol_inv, contract_t, precision=precise_mode)
    col_factor = lax.dot_general(col_rows, chol_inv, contract_t, precision=precise_mode)
    product = lax.dot_general(slab_factor, col_factor, contract_t, precision=precise_mode)
    device_rows = trailing.shape[1]
    cols_dev = trailing.shape[2]
    column_ids = lax.axis_index("row") * cols_dev + jnp.arange(cols_dev, dtype=jnp.int32)
    update = jnp.where(
        column_ids[None, :] < front_order[0], trailing[0] - product, jnp.float32(0.0)
    )
    block_rows = device_rows // BS
    block_cols = cols_dev // BS
    blocks = (
        update.reshape(block_rows, BS, block_cols, BS)
        .transpose(0, 2, 1, 3)
        .reshape(block_rows * block_cols, BS * BS)
    )
    nblocks = block_rows * block_cols
    groups = lax.axis_size("cube")
    own_group = lax.axis_index("cube")
    dest_all = dest_group[:, 0, 0, :, 0]
    parent_all = parent_block[:, 0, 0, :, 0]
    dest_mine = lax.dynamic_index_in_dim(dest_all, own_group, 0, keepdims=False)
    parent_rows = parent_front.shape[1]
    parent_brows = parent_rows // BS
    nparent = parent_brows * block_cols
    capacity = 2 * nblocks // groups
    hit_table = (dest_mine[:, None] == jnp.arange(groups, dtype=jnp.int32)[None, :]).astype(
        jnp.int32
    )
    before = jnp.cumsum(hit_table, axis=0) - hit_table
    slot_ids = jnp.sum(before * hit_table, axis=1)
    position = dest_mine * capacity + slot_ids
    picker = (position[None, :] == jnp.arange(groups * capacity, dtype=jnp.int32)[:, None]).astype(
        jnp.float32
    )
    outgoing = jnp.dot(picker, blocks, precision=precise_mode).reshape(groups, capacity, BS * BS)
    incoming = lax.all_to_all(outgoing, "cube", split_axis=0, concat_axis=0, tiled=True)
    arriving = (dest_all == own_group).astype(jnp.int32)
    rank_ids = jnp.cumsum(arriving, axis=1) - arriving
    in_slot = (
        arriving[:, :, None]
        * (rank_ids[:, :, None] == jnp.arange(capacity, dtype=jnp.int32)[None, None, :])
    ).astype(jnp.float32)
    to_parent = (
        parent_all[:, :, None] == jnp.arange(nparent, dtype=jnp.int32)[None, None, :]
    ).astype(jnp.float32)
    weight = jnp.einsum("sbk,sbp->psk", in_slot, to_parent, precision=precise_mode)
    assembled = jnp.dot(
        weight.reshape(nparent, groups * capacity),
        incoming.reshape(groups * capacity, BS * BS),
        precision=precise_mode,
    )
    assembled = (
        assembled.reshape(parent_brows, block_cols, BS, BS)
        .transpose(0, 2, 1, 3)
        .reshape(parent_rows, cols_dev)
    )
    return (parent_front[0] + assembled)[None]


def solution(mesh):
    placed = (
        P("cube", None, None),
        P("cube", ("row", "col"), None),
        P("cube", "col", "row"),
        P("cube", "col", "row"),
        P("cube"),
        P(None, "col", "row", None, None),
        P(None, "col", "row", None, None),
    )
    return jax.shard_map(
        shards, mesh=mesh, in_specs=placed, out_specs=P("cube", "col", "row"), check_vma=False
    )
```

```python
import functools

import jax
import jax.numpy as jnp
from jax import lax
from jax.experimental import pallas as pl
from jax.experimental.pallas import tpu as pltpu
from jax.sharding import PartitionSpec as P

BS = 128


def spread(value, axis, root):
    mine = lax.axis_index(axis) == root
    return lax.psum(jnp.where(mine, value, jnp.zeros_like(value)), axis)


def shards(diag_block, panel, trailing, parent_front, front_order, dest_group, parent_block):
    precise_mode = lax.Precision.HIGHEST
    slab_rows = spread(panel[0], "row", 0)
    col_rows = lax.all_gather(panel[0], "col", axis=0, tiled=True)
    chol_diag = jnp.linalg.cholesky(diag_block[0])
    order = chol_diag.shape[0]
    chol_inv = lax.linalg.triangular_solve(
        chol_diag, jnp.eye(order, dtype=chol_diag.dtype), left_side=True, lower=True
    )
    contract_t = (((1,), (1,)), ((), ()))
    slab_factor = lax.dot_general(slab_rows, chol_inv, contract_t, precision=precise_mode)
    col_factor = lax.dot_general(col_rows, chol_inv, contract_t, precision=precise_mode)
    product = lax.dot_general(slab_factor, col_factor, contract_t, precision=precise_mode)
    device_rows = trailing.shape[1]
    cols_dev = trailing.shape[2]
    column_ids = lax.axis_index("row") * cols_dev + jnp.arange(cols_dev, dtype=jnp.int32)
    update = jnp.where(
        column_ids[None, :] < front_order[0], trailing[0] - product, jnp.float32(0.0)
    )
    block_rows = device_rows // BS
    block_cols = cols_dev // BS
    nblocks = block_rows * block_cols
    groups = lax.axis_size("cube")
    own_group = lax.axis_index("cube")
    dest_all = dest_group[:, 0, 0, :, 0]
    parent_all = parent_block[:, 0, 0, :, 0]
    dest_mine = lax.dynamic_index_in_dim(dest_all, own_group, 0, keepdims=False)
    capacity = 2 * nblocks // groups
    nslots = groups * capacity
    hit_table = (dest_mine[:, None] == jnp.arange(groups, dtype=jnp.int32)[None, :]).astype(
        jnp.int32
    )
    before = jnp.cumsum(hit_table, axis=0) - hit_table
    slot_ids = jnp.sum(before * hit_table, axis=1)
    position = dest_mine * capacity + slot_ids
    source_of_slot = (
        jnp.full((nslots,), -1, jnp.int32)
        .at[position]
        .set(jnp.arange(nblocks, dtype=jnp.int32), mode="drop")
    )
    outgoing = pack_blocks(source_of_slot, update, block_cols)
    incoming = lax.all_to_all(
        outgoing.reshape(groups, capacity * BS, BS), "cube", split_axis=0, concat_axis=0, tiled=True
    )
    arriving = dest_all == own_group
    arriving_i = arriving.astype(jnp.int32)
    rank_ids = jnp.cumsum(arriving_i, axis=1) - arriving_i
    in_position = jnp.where(
        arriving,
        jnp.arange(groups, dtype=jnp.int32)[:, None] * capacity + rank_ids,
        nslots,
    )
    parent_of_slot = (
        jnp.full((nslots,), -1, jnp.int32)
        .at[in_position.reshape(-1)]
        .set(parent_all.reshape(-1), mode="drop")
    )
    assembled = combine_blocks(parent_of_slot, incoming.reshape(nslots, BS, BS), parent_front[0])
    return assembled[None]


def pack_kernel(block_cols, source_ref, update_ref, out_ref):
    def body(slot, carry):
        block = source_ref[slot]
        live = block >= 0
        block = jnp.maximum(block, 0)
        rows = pl.ds(pl.multiple_of((block // block_cols) * BS, BS), BS)
        cols = pl.ds(pl.multiple_of((block % block_cols) * BS, BS), BS)
        out_ref[slot] = jnp.where(live, update_ref[rows, cols], jnp.float32(0.0))
        return carry

    lax.fori_loop(0, out_ref.shape[0], body, 0)


def pack_blocks(source_of_slot, update, block_cols):
    nslots = source_of_slot.shape[0]
    return pl.pallas_call(
        functools.partial(pack_kernel, block_cols),
        out_shape=jax.ShapeDtypeStruct((nslots, BS, BS), update.dtype),
        in_specs=[
            pl.BlockSpec(memory_space=pltpu.SMEM),
            pl.BlockSpec(memory_space=pltpu.VMEM),
        ],
        out_specs=pl.BlockSpec(memory_space=pltpu.VMEM),
    )(source_of_slot, update)


def combine_kernel(parent_ref, incoming_ref, front_ref, out_ref):
    out_ref[...] = front_ref[...]

    def body(slot, carry):
        parent = parent_ref[slot]

        @pl.when(parent >= 0)
        def _():
            cols = pl.ds(pl.multiple_of(parent * BS, BS), BS)
            out_ref[:, cols] = out_ref[:, cols] + incoming_ref[slot]

        return carry

    lax.fori_loop(0, incoming_ref.shape[0], body, 0)


def combine_blocks(parent_of_slot, incoming, front):
    return pl.pallas_call(
        combine_kernel,
        out_shape=jax.ShapeDtypeStruct(front.shape, front.dtype),
        in_specs=[
            pl.BlockSpec(memory_space=pltpu.SMEM),
            pl.BlockSpec(memory_space=pltpu.VMEM),
            pl.BlockSpec(memory_space=pltpu.VMEM),
        ],
        out_specs=pl.BlockSpec(memory_space=pltpu.VMEM),
    )(parent_of_slot, incoming, front)


def solution(mesh):
    placed = (
        P("cube", None, None),
        P("cube", ("row", "col"), None),
        P("cube", "col", "row"),
        P("cube", "col", "row"),
        P("cube"),
        P(None, "col", "row", None, None),
        P(None, "col", "row", None, None),
    )
    return jax.shard_map(
        shards, mesh=mesh, in_specs=placed, out_specs=P("cube", "col", "row"), check_vma=False
    )
```

```python
import functools

import jax
import jax.numpy as jnp
from jax import lax
from jax.experimental import pallas as pl
from jax.experimental.pallas import tpu as pltpu
from jax.sharding import PartitionSpec as P

BS = 128


def spread(value, axis, root):
    mine = lax.axis_index(axis) == root
    return lax.psum(jnp.where(mine, value, jnp.zeros_like(value)), axis)


def shards(diag_block, panel, trailing, parent_front, front_order, dest_group, parent_block):
    precise_mode = lax.Precision.HIGHEST
    slab_rows = spread(panel[0], "row", 0)
    col_rows = lax.all_gather(panel[0], "col", axis=0, tiled=True)
    chol_inv = factor_inverse(diag_block[0])
    contract_t = (((1,), (1,)), ((), ()))
    slab_factor = lax.dot_general(slab_rows, chol_inv, contract_t, precision=precise_mode)
    col_factor = lax.dot_general(col_rows, chol_inv, contract_t, precision=precise_mode)
    product = lax.dot_general(slab_factor, col_factor, contract_t, precision=precise_mode)
    device_rows = trailing.shape[1]
    cols_dev = trailing.shape[2]
    column_ids = lax.axis_index("row") * cols_dev + jnp.arange(cols_dev, dtype=jnp.int32)
    update = jnp.where(
        column_ids[None, :] < front_order[0], trailing[0] - product, jnp.float32(0.0)
    )
    block_rows = device_rows // BS
    block_cols = cols_dev // BS
    nblocks = block_rows * block_cols
    groups = lax.axis_size("cube")
    own_group = lax.axis_index("cube")
    dest_all = dest_group[:, 0, 0, :, 0]
    parent_all = parent_block[:, 0, 0, :, 0]
    dest_mine = lax.dynamic_index_in_dim(dest_all, own_group, 0, keepdims=False)
    capacity = 2 * nblocks // groups
    nslots = groups * capacity
    hit_table = (dest_mine[:, None] == jnp.arange(groups, dtype=jnp.int32)[None, :]).astype(
        jnp.int32
    )
    before = jnp.cumsum(hit_table, axis=0) - hit_table
    slot_ids = jnp.sum(before * hit_table, axis=1)
    position = dest_mine * capacity + slot_ids
    source_of_slot = (
        jnp.full((nslots,), -1, jnp.int32)
        .at[position]
        .set(jnp.arange(nblocks, dtype=jnp.int32), mode="drop")
    )
    outgoing = pack_blocks(source_of_slot, update, block_cols)
    incoming = lax.all_to_all(
        outgoing.reshape(groups, capacity * BS, BS), "cube", split_axis=0, concat_axis=0, tiled=True
    )
    arriving = dest_all == own_group
    arriving_i = arriving.astype(jnp.int32)
    rank_ids = jnp.cumsum(arriving_i, axis=1) - arriving_i
    in_position = jnp.where(
        arriving,
        jnp.arange(groups, dtype=jnp.int32)[:, None] * capacity + rank_ids,
        nslots,
    )
    parent_of_slot = (
        jnp.full((nslots,), -1, jnp.int32)
        .at[in_position.reshape(-1)]
        .set(parent_all.reshape(-1), mode="drop")
    )
    assembled = combine_blocks(parent_of_slot, incoming.reshape(nslots, BS, BS), parent_front[0])
    return assembled[None]


def pack_kernel(block_cols, source_ref, update_ref, out_ref):
    def body(slot, carry):
        block = source_ref[slot]
        live = block >= 0
        block = jnp.maximum(block, 0)
        rows = pl.ds(pl.multiple_of((block // block_cols) * BS, BS), BS)
        cols = pl.ds(pl.multiple_of((block % block_cols) * BS, BS), BS)
        out_ref[slot] = jnp.where(live, update_ref[rows, cols], jnp.float32(0.0))
        return carry

    lax.fori_loop(0, out_ref.shape[0], body, 0)


def pack_blocks(source_of_slot, update, block_cols):
    nslots = source_of_slot.shape[0]
    return pl.pallas_call(
        functools.partial(pack_kernel, block_cols),
        out_shape=jax.ShapeDtypeStruct((nslots, BS, BS), update.dtype),
        in_specs=[
            pl.BlockSpec(memory_space=pltpu.SMEM),
            pl.BlockSpec(memory_space=pltpu.VMEM),
        ],
        out_specs=pl.BlockSpec(memory_space=pltpu.VMEM),
    )(source_of_slot, update)


def combine_kernel(parent_ref, incoming_ref, front_ref, out_ref):
    out_ref[...] = front_ref[...]

    def body(slot, carry):
        parent = parent_ref[slot]

        @pl.when(parent >= 0)
        def _():
            cols = pl.ds(pl.multiple_of(parent * BS, BS), BS)
            out_ref[:, cols] = out_ref[:, cols] + incoming_ref[slot]

        return carry

    lax.fori_loop(0, incoming_ref.shape[0], body, 0)


def combine_blocks(parent_of_slot, incoming, front):
    return pl.pallas_call(
        combine_kernel,
        out_shape=jax.ShapeDtypeStruct(front.shape, front.dtype),
        in_specs=[
            pl.BlockSpec(memory_space=pltpu.SMEM),
            pl.BlockSpec(memory_space=pltpu.VMEM),
            pl.BlockSpec(memory_space=pltpu.VMEM),
        ],
        out_specs=pl.BlockSpec(memory_space=pltpu.VMEM),
    )(parent_of_slot, incoming, front)


def factor_kernel(a_ref, inv_ref, work_ref, g_ref):
    n = a_ref.shape[0]
    nb = n // BS
    hp = lax.Precision.HIGHEST
    nt = (((1,), (1,)), ((), ()))
    work_ref[...] = a_ref[...]
    lane = lax.broadcasted_iota(jnp.int32, (1, 2 * BS), 1)
    sub = lax.broadcasted_iota(jnp.int32, (BS, BS), 0)
    col = lax.broadcasted_iota(jnp.int32, (BS, BS), 1)
    eye = (sub == col).astype(jnp.float32)
    diag_inv = []
    for k in range(nb):
        kk = pl.ds(k * BS, BS)
        g_ref[:, :BS] = work_ref[kk, kk]
        g_ref[:, BS:] = eye

        def step(j, carry):
            row = g_ref[pl.ds(j, 1), :]
            pivot = jnp.sum(jnp.where(lane == j, row, 0.0), axis=1, keepdims=True)
            scaled = row / jnp.sqrt(pivot)
            down = jnp.where(lane[:, :BS] > j, scaled[:, :BS], 0.0)
            down_col = jnp.transpose(jnp.broadcast_to(down, (BS, BS)))
            g = g_ref[...]
            g_ref[:, :BS] = g[:, :BS] - down_col * scaled[:, :BS]
            g_ref[:, BS:] = g[:, BS:] - down_col * scaled[:, BS:]
            g_ref[pl.ds(j, 1), :] = scaled
            return carry

        lax.fori_loop(0, BS, step, 0)
        upper = jnp.where(col >= sub, g_ref[:, :BS], 0.0)
        lk_inv = g_ref[:, BS:]
        diag_inv.append(lk_inv)
        work_ref[kk, kk] = jnp.transpose(upper)
        if k < nb - 1:
            rest = pl.ds((k + 1) * BS, n - (k + 1) * BS)
            panel = lax.dot_general(work_ref[rest, kk], lk_inv, nt, precision=hp,
                                    preferred_element_type=jnp.float32)
            work_ref[rest, kk] = panel
            work_ref[rest, rest] = work_ref[rest, rest] - lax.dot_general(
                panel, panel, nt, precision=hp, preferred_element_type=jnp.float32)
    inv_ref[...] = jnp.zeros_like(inv_ref)
    inv_ref[pl.ds(0, BS), pl.ds(0, BS)] = diag_inv[0]
    for i in range(1, nb):
        ii = pl.ds(i * BS, BS)
        left = pl.ds(0, i * BS)
        mixed = jnp.dot(work_ref[ii, left], inv_ref[left, left], precision=hp,
                        preferred_element_type=jnp.float32)
        inv_ref[ii, left] = -jnp.dot(diag_inv[i], mixed, precision=hp,
                                     preferred_element_type=jnp.float32)
        inv_ref[ii, ii] = diag_inv[i]


def factor_inverse(a):
    n = a.shape[0]
    return pl.pallas_call(
        factor_kernel,
        out_shape=jax.ShapeDtypeStruct((n, n), a.dtype),
        in_specs=[pl.BlockSpec(memory_space=pltpu.VMEM)],
        out_specs=pl.BlockSpec(memory_space=pltpu.VMEM),
        scratch_shapes=[pltpu.VMEM((n, n), jnp.float32), pltpu.VMEM((BS, 2 * BS), jnp.float32)],
    )(a)

def solution(mesh):
    placed = (
        P("cube", None, None),
        P("cube", ("row", "col"), None),
        P("cube", "col", "row"),
        P("cube", "col", "row"),
        P("cube"),
        P(None, "col", "row", None, None),
        P(None, "col", "row", None, None),
    )
    return jax.shard_map(
        shards, mesh=mesh, in_specs=placed, out_specs=P("cube", "col", "row"), check_vma=False
    )
```

```python
import functools

import jax
import jax.numpy as jnp
from jax import lax
from jax.experimental import pallas as pl
from jax.experimental.pallas import tpu as pltpu
from jax.sharding import PartitionSpec as P

BS = 128


def spread(value, axis, root):
    mine = lax.axis_index(axis) == root
    return lax.psum(jnp.where(mine, value, jnp.zeros_like(value)), axis)


def shards(diag_block, panel, trailing, parent_front, front_order, dest_group, parent_block):
    precise_mode = lax.Precision.HIGHEST
    slab_rows = spread(panel[0], "row", 0)
    col_rows = lax.all_gather(panel[0], "col", axis=0, tiled=True)
    chol_inv = factor_inverse(diag_block[0])
    contract_t = (((1,), (1,)), ((), ()))
    slab_factor = lax.dot_general(slab_rows, chol_inv, contract_t, precision=precise_mode)
    col_factor = lax.dot_general(col_rows, chol_inv, contract_t, precision=precise_mode)
    product = lax.dot_general(slab_factor, col_factor, contract_t, precision=precise_mode)
    device_rows = trailing.shape[1]
    cols_dev = trailing.shape[2]
    column_ids = lax.axis_index("row") * cols_dev + jnp.arange(cols_dev, dtype=jnp.int32)
    update = jnp.where(
        column_ids[None, :] < front_order[0], trailing[0] - product, jnp.float32(0.0)
    )
    block_rows = device_rows // BS
    block_cols = cols_dev // BS
    nblocks = block_rows * block_cols
    groups = lax.axis_size("cube")
    own_group = lax.axis_index("cube")
    dest_all = dest_group[:, 0, 0, :, 0]
    parent_all = parent_block[:, 0, 0, :, 0]
    dest_mine = lax.dynamic_index_in_dim(dest_all, own_group, 0, keepdims=False)
    capacity = 2 * nblocks // groups
    nslots = groups * capacity
    hit_table = (dest_mine[:, None] == jnp.arange(groups, dtype=jnp.int32)[None, :]).astype(
        jnp.int32
    )
    before = jnp.cumsum(hit_table, axis=0) - hit_table
    slot_ids = jnp.sum(before * hit_table, axis=1)
    position = dest_mine * capacity + slot_ids
    source_of_slot = (
        jnp.full((nslots,), -1, jnp.int32)
        .at[position]
        .set(jnp.arange(nblocks, dtype=jnp.int32), mode="drop")
    )
    outgoing = pack_blocks(source_of_slot, update, block_cols)
    incoming = lax.all_to_all(
        outgoing.reshape(groups, capacity * BS, BS), "cube", split_axis=0, concat_axis=0, tiled=True
    )
    arriving = dest_all == own_group
    arriving_i = arriving.astype(jnp.int32)
    rank_ids = jnp.cumsum(arriving_i, axis=1) - arriving_i
    in_position = jnp.where(
        arriving,
        jnp.arange(groups, dtype=jnp.int32)[:, None] * capacity + rank_ids,
        nslots,
    )
    parent_of_slot = (
        jnp.full((nslots,), -1, jnp.int32)
        .at[in_position.reshape(-1)]
        .set(parent_all.reshape(-1), mode="drop")
    )
    assembled = combine_blocks(parent_of_slot, incoming.reshape(nslots, BS, BS), parent_front[0])
    return assembled[None]


def pack_kernel(block_cols, source_ref, update_ref, out_ref):
    def body(slot, carry):
        block = source_ref[slot]
        live = block >= 0
        block = jnp.maximum(block, 0)
        rows = pl.ds(pl.multiple_of((block // block_cols) * BS, BS), BS)
        cols = pl.ds(pl.multiple_of((block % block_cols) * BS, BS), BS)
        out_ref[slot] = jnp.where(live, update_ref[rows, cols], jnp.float32(0.0))
        return carry

    lax.fori_loop(0, out_ref.shape[0], body, 0)


def pack_blocks(source_of_slot, update, block_cols):
    nslots = source_of_slot.shape[0]
    return pl.pallas_call(
        functools.partial(pack_kernel, block_cols),
        out_shape=jax.ShapeDtypeStruct((nslots, BS, BS), update.dtype),
        in_specs=[
            pl.BlockSpec(memory_space=pltpu.SMEM),
            pl.BlockSpec(memory_space=pltpu.VMEM),
        ],
        out_specs=pl.BlockSpec(memory_space=pltpu.VMEM),
    )(source_of_slot, update)


def combine_kernel(parent_ref, incoming_ref, front_ref, out_ref):
    out_ref[...] = front_ref[...]

    def body(slot, carry):
        parent = parent_ref[slot]

        @pl.when(parent >= 0)
        def _():
            cols = pl.ds(pl.multiple_of(parent * BS, BS), BS)
            out_ref[:, cols] = out_ref[:, cols] + incoming_ref[slot]

        return carry

    lax.fori_loop(0, incoming_ref.shape[0], body, 0)


def combine_blocks(parent_of_slot, incoming, front):
    return pl.pallas_call(
        combine_kernel,
        out_shape=jax.ShapeDtypeStruct(front.shape, front.dtype),
        in_specs=[
            pl.BlockSpec(memory_space=pltpu.SMEM),
            pl.BlockSpec(memory_space=pltpu.VMEM),
            pl.BlockSpec(memory_space=pltpu.VMEM),
        ],
        out_specs=pl.BlockSpec(memory_space=pltpu.VMEM),
    )(parent_of_slot, incoming, front)


def factor_kernel(a_ref, inv_ref, work_ref, g_ref):
    n = a_ref.shape[0]
    nb = n // BS
    hp = lax.Precision.HIGHEST
    nt = (((1,), (1,)), ((), ()))
    work_ref[...] = a_ref[...]
    lane = lax.broadcasted_iota(jnp.int32, (1, 2 * BS), 1)
    sub = lax.broadcasted_iota(jnp.int32, (BS, BS), 0)
    col = lax.broadcasted_iota(jnp.int32, (BS, BS), 1)
    eye = (sub == col).astype(jnp.float32)
    diag_inv = []
    for k in range(nb):
        kk = pl.ds(k * BS, BS)
        g_ref[:, :BS] = work_ref[kk, kk]
        g_ref[:, BS:] = eye

        for lo in range(0, BS, 8):
            height = BS - lo
            rid = lo + lax.broadcasted_iota(jnp.int32, (height, 1), 0)

            def step(j, carry, lo=lo, rid=rid):
                row = g_ref[pl.ds(j, 1), :]
                pivot = jnp.sum(jnp.where(lane == j, row, 0.0), axis=1, keepdims=True)
                inv_d = 1.0 / jnp.sqrt(pivot)
                scaled = row * inv_d
                live = g_ref[lo:, :]
                column = jnp.sum(
                    jnp.where(lane[:, :BS] == j, live[:, :BS], 0.0), axis=1, keepdims=True
                )
                down = jnp.where(rid > j, column * inv_d, 0.0)
                g_ref[lo:, :] = live - down * scaled
                g_ref[pl.ds(j, 1), :] = scaled
                return carry

            lax.fori_loop(lo, lo + 8, step, 0, unroll=2)
        upper = jnp.where(col >= sub, g_ref[:, :BS], 0.0)
        lk_inv = g_ref[:, BS:]
        diag_inv.append(lk_inv)
        work_ref[kk, kk] = jnp.transpose(upper)
        if k < nb - 1:
            rest = pl.ds((k + 1) * BS, n - (k + 1) * BS)
            panel = lax.dot_general(work_ref[rest, kk], lk_inv, nt, precision=hp,
                                    preferred_element_type=jnp.float32)
            work_ref[rest, kk] = panel
            work_ref[rest, rest] = work_ref[rest, rest] - lax.dot_general(
                panel, panel, nt, precision=hp, preferred_element_type=jnp.float32)
    inv_ref[...] = jnp.zeros_like(inv_ref)
    inv_ref[pl.ds(0, BS), pl.ds(0, BS)] = diag_inv[0]
    for i in range(1, nb):
        ii = pl.ds(i * BS, BS)
        left = pl.ds(0, i * BS)
        mixed = jnp.dot(work_ref[ii, left], inv_ref[left, left], precision=hp,
                        preferred_element_type=jnp.float32)
        inv_ref[ii, left] = -jnp.dot(diag_inv[i], mixed, precision=hp,
                                     preferred_element_type=jnp.float32)
        inv_ref[ii, ii] = diag_inv[i]


def factor_inverse(a):
    n = a.shape[0]
    return pl.pallas_call(
        factor_kernel,
        out_shape=jax.ShapeDtypeStruct((n, n), a.dtype),
        in_specs=[pl.BlockSpec(memory_space=pltpu.VMEM)],
        out_specs=pl.BlockSpec(memory_space=pltpu.VMEM),
        scratch_shapes=[pltpu.VMEM((n, n), jnp.float32), pltpu.VMEM((BS, 2 * BS), jnp.float32)],
    )(a)

def solution(mesh):
    placed = (
        P("cube", None, None),
        P("cube", ("row", "col"), None),
        P("cube", "col", "row"),
        P("cube", "col", "row"),
        P("cube"),
        P(None, "col", "row", None, None),
        P(None, "col", "row", None, None),
    )
    return jax.shard_map(
        shards, mesh=mesh, in_specs=placed, out_specs=P("cube", "col", "row"), check_vma=False
    )
```

```python
import functools

import jax
import jax.numpy as jnp
from jax import lax
from jax.experimental import pallas as pl
from jax.experimental.pallas import tpu as pltpu
from jax.sharding import PartitionSpec as P

BS = 128
STRIP = 32


def spread(value, axis, root):
    mine = lax.axis_index(axis) == root
    return lax.psum(jnp.where(mine, value, jnp.zeros_like(value)), axis)


def shards(diag_block, panel, trailing, parent_front, front_order, dest_group, parent_block):
    precise_mode = lax.Precision.HIGHEST
    slab_rows = spread(panel[0], "row", 0)
    col_rows = lax.all_gather(panel[0], "col", axis=0, tiled=True)
    chol_inv = factor_inverse(diag_block[0])
    contract_t = (((1,), (1,)), ((), ()))
    slab_factor = lax.dot_general(slab_rows, chol_inv, contract_t, precision=precise_mode)
    slab_solved = jnp.dot(slab_factor, chol_inv, precision=precise_mode)
    product = lax.dot_general(slab_solved, col_rows, contract_t, precision=precise_mode)
    device_rows = trailing.shape[1]
    cols_dev = trailing.shape[2]
    column_ids = lax.axis_index("row") * cols_dev + jnp.arange(cols_dev, dtype=jnp.int32)
    update = jnp.where(
        column_ids[None, :] < front_order[0], trailing[0] - product, jnp.float32(0.0)
    )
    block_rows = device_rows // BS
    block_cols = cols_dev // BS
    nblocks = block_rows * block_cols
    groups = lax.axis_size("cube")
    own_group = lax.axis_index("cube")
    dest_all = dest_group[:, 0, 0, :, 0]
    parent_all = parent_block[:, 0, 0, :, 0]
    dest_mine = lax.dynamic_index_in_dim(dest_all, own_group, 0, keepdims=False)
    capacity = 2 * nblocks // groups
    nslots = groups * capacity
    hit_table = (dest_mine[:, None] == jnp.arange(groups, dtype=jnp.int32)[None, :]).astype(
        jnp.int32
    )
    before = jnp.cumsum(hit_table, axis=0) - hit_table
    slot_ids = jnp.sum(before * hit_table, axis=1)
    position = dest_mine * capacity + slot_ids
    source_of_slot = (
        jnp.full((nslots,), -1, jnp.int32)
        .at[position]
        .set(jnp.arange(nblocks, dtype=jnp.int32), mode="drop")
    )
    outgoing = pack_blocks(source_of_slot, update, block_cols)
    incoming = lax.all_to_all(
        outgoing.reshape(groups, capacity * BS, BS), "cube", split_axis=0, concat_axis=0, tiled=True
    )
    arriving = dest_all == own_group
    arriving_i = arriving.astype(jnp.int32)
    rank_ids = jnp.cumsum(arriving_i, axis=1) - arriving_i
    in_position = jnp.where(
        arriving,
        jnp.arange(groups, dtype=jnp.int32)[:, None] * capacity + rank_ids,
        nslots,
    )
    parent_of_slot = (
        jnp.full((nslots,), -1, jnp.int32)
        .at[in_position.reshape(-1)]
        .set(parent_all.reshape(-1), mode="drop")
    )
    assembled = combine_blocks(parent_of_slot, incoming.reshape(nslots, BS, BS), parent_front[0])
    return assembled[None]


def pack_kernel(block_cols, source_ref, update_ref, out_ref):
    def body(slot, carry):
        block = source_ref[slot]
        live = block >= 0
        block = jnp.maximum(block, 0)
        rows = pl.ds(pl.multiple_of((block // block_cols) * BS, BS), BS)
        cols = pl.ds(pl.multiple_of((block % block_cols) * BS, BS), BS)
        out_ref[slot] = jnp.where(live, update_ref[rows, cols], jnp.float32(0.0))
        return carry

    lax.fori_loop(0, out_ref.shape[0], body, 0)


def pack_blocks(source_of_slot, update, block_cols):
    nslots = source_of_slot.shape[0]
    return pl.pallas_call(
        functools.partial(pack_kernel, block_cols),
        out_shape=jax.ShapeDtypeStruct((nslots, BS, BS), update.dtype),
        in_specs=[
            pl.BlockSpec(memory_space=pltpu.SMEM),
            pl.BlockSpec(memory_space=pltpu.VMEM),
        ],
        out_specs=pl.BlockSpec(memory_space=pltpu.VMEM),
    )(source_of_slot, update)


def combine_kernel(parent_ref, incoming_ref, front_ref, out_ref):
    out_ref[...] = front_ref[...]

    def body(slot, carry):
        parent = parent_ref[slot]

        @pl.when(parent >= 0)
        def _():
            cols = pl.ds(pl.multiple_of(parent * BS, BS), BS)
            out_ref[:, cols] = out_ref[:, cols] + incoming_ref[slot]

        return carry

    lax.fori_loop(0, incoming_ref.shape[0], body, 0)


def combine_blocks(parent_of_slot, incoming, front):
    return pl.pallas_call(
        combine_kernel,
        out_shape=jax.ShapeDtypeStruct(front.shape, front.dtype),
        in_specs=[
            pl.BlockSpec(memory_space=pltpu.SMEM),
            pl.BlockSpec(memory_space=pltpu.VMEM),
            pl.BlockSpec(memory_space=pltpu.VMEM),
        ],
        out_specs=pl.BlockSpec(memory_space=pltpu.VMEM),
    )(parent_of_slot, incoming, front)


def factor_kernel(a_ref, inv_ref, work_ref, g_ref):
    n = a_ref.shape[0]
    nb = n // BS
    hp = lax.Precision.HIGHEST
    nt = (((1,), (1,)), ((), ()))
    work_ref[...] = a_ref[...]
    lane = lax.broadcasted_iota(jnp.int32, (1, 2 * BS), 1)
    sub = lax.broadcasted_iota(jnp.int32, (BS, BS), 0)
    col = lax.broadcasted_iota(jnp.int32, (BS, BS), 1)
    eye = (sub == col).astype(jnp.float32)
    diag_inv = []
    for k in range(nb):
        kk = pl.ds(k * BS, BS)
        g_ref[:, :BS] = work_ref[kk, kk]
        g_ref[:, BS:] = eye

        for strip in range(0, BS, STRIP):
            for lo in range(strip, strip + STRIP, 8):
                height = strip + STRIP - lo
                rid = lo + lax.broadcasted_iota(jnp.int32, (height, 1), 0)

                def step(j, carry, lo=lo, rid=rid, end=strip + STRIP):
                    row = g_ref[pl.ds(j, 1), :]
                    pivot = jnp.sum(jnp.where(lane == j, row, 0.0), axis=1, keepdims=True)
                    inv_d = 1.0 / jnp.sqrt(pivot)
                    scaled = row * inv_d
                    live = g_ref[lo:end, :]
                    column = jnp.sum(
                        jnp.where(lane[:, :BS] == j, live[:, :BS], 0.0), axis=1, keepdims=True
                    )
                    down = jnp.where(rid > j, column * inv_d, 0.0)
                    g_ref[lo:end, :] = live - down * scaled
                    g_ref[pl.ds(j, 1), :] = scaled
                    return carry

                lax.fori_loop(lo, lo + 8, step, 0, unroll=2)
            below = strip + STRIP
            if below < BS:
                done = g_ref[strip:below, :]
                mult = jnp.transpose(done[:, :BS])[below:, :]
                g_ref[below:, :] = g_ref[below:, :] - jnp.dot(
                    mult, done, precision=hp, preferred_element_type=jnp.float32
                )
        upper = jnp.where(col >= sub, g_ref[:, :BS], 0.0)
        lk_inv = g_ref[:, BS:]
        diag_inv.append(lk_inv)
        work_ref[kk, kk] = jnp.transpose(upper)
        if k < nb - 1:
            rest = pl.ds((k + 1) * BS, n - (k + 1) * BS)
            panel = lax.dot_general(work_ref[rest, kk], lk_inv, nt, precision=hp,
                                    preferred_element_type=jnp.float32)
            work_ref[rest, kk] = panel
            work_ref[rest, rest] = work_ref[rest, rest] - lax.dot_general(
                panel, panel, nt, precision=hp, preferred_element_type=jnp.float32)
    inv_ref[...] = jnp.zeros_like(inv_ref)
    inv_ref[pl.ds(0, BS), pl.ds(0, BS)] = diag_inv[0]
    for i in range(1, nb):
        ii = pl.ds(i * BS, BS)
        left = pl.ds(0, i * BS)
        mixed = jnp.dot(work_ref[ii, left], inv_ref[left, left], precision=hp,
                        preferred_element_type=jnp.float32)
        inv_ref[ii, left] = -jnp.dot(diag_inv[i], mixed, precision=hp,
                                     preferred_element_type=jnp.float32)
        inv_ref[ii, ii] = diag_inv[i]


def factor_inverse(a):
    n = a.shape[0]
    return pl.pallas_call(
        factor_kernel,
        out_shape=jax.ShapeDtypeStruct((n, n), a.dtype),
        in_specs=[pl.BlockSpec(memory_space=pltpu.VMEM)],
        out_specs=pl.BlockSpec(memory_space=pltpu.VMEM),
        scratch_shapes=[pltpu.VMEM((n, n), jnp.float32), pltpu.VMEM((BS, 2 * BS), jnp.float32)],
    )(a)

def solution(mesh):
    placed = (
        P("cube", None, None),
        P("cube", ("row", "col"), None),
        P("cube", "col", "row"),
        P("cube", "col", "row"),
        P("cube"),
        P(None, "col", "row", None, None),
        P(None, "col", "row", None, None),
    )
    return jax.shard_map(
        shards, mesh=mesh, in_specs=placed, out_specs=P("cube", "col", "row"), check_vma=False
    )
```

```python
import functools

import jax
import jax.numpy as jnp
from jax import lax
from jax.experimental import pallas as pl
from jax.experimental.pallas import tpu as pltpu
from jax.sharding import PartitionSpec as P

BS = 128
STRIP = 32


def spread(value, axis, root):
    mine = lax.axis_index(axis) == root
    return lax.psum(jnp.where(mine, value, jnp.zeros_like(value)), axis)


def shards(diag_block, panel, trailing, parent_front, front_order, dest_group, parent_block):
    precise_mode = lax.Precision.HIGHEST
    slab_rows = spread(panel[0], "row", 0)
    col_rows = lax.all_gather(panel[0], "col", axis=0, tiled=True)
    chol_inv = factor_inverse(diag_block[0])
    contract_t = (((1,), (1,)), ((), ()))
    slab_factor = lax.dot_general(slab_rows, chol_inv, contract_t, precision=precise_mode)
    slab_solved = jnp.dot(slab_factor, chol_inv, precision=precise_mode)
    product = lax.dot_general(slab_solved, col_rows, contract_t, precision=precise_mode)
    device_rows = trailing.shape[1]
    cols_dev = trailing.shape[2]
    column_ids = lax.axis_index("row") * cols_dev + jnp.arange(cols_dev, dtype=jnp.int32)
    update = jnp.where(
        column_ids[None, :] < front_order[0], trailing[0] - product, jnp.float32(0.0)
    )
    block_rows = device_rows // BS
    block_cols = cols_dev // BS
    nblocks = block_rows * block_cols
    groups = lax.axis_size("cube")
    own_group = lax.axis_index("cube")
    dest_all = dest_group[:, 0, 0, :, 0]
    parent_all = parent_block[:, 0, 0, :, 0]
    dest_mine = lax.dynamic_index_in_dim(dest_all, own_group, 0, keepdims=False)
    capacity = 2 * nblocks // groups
    nslots = groups * capacity
    hit_table = (dest_mine[:, None] == jnp.arange(groups, dtype=jnp.int32)[None, :]).astype(
        jnp.int32
    )
    before = jnp.cumsum(hit_table, axis=0) - hit_table
    slot_ids = jnp.sum(before * hit_table, axis=1)
    position = dest_mine * capacity + slot_ids
    source_of_slot = (
        jnp.full((nslots,), -1, jnp.int32)
        .at[position]
        .set(jnp.arange(nblocks, dtype=jnp.int32), mode="drop")
    )
    outgoing = pack_blocks(source_of_slot, update, block_cols)
    incoming = lax.all_to_all(
        outgoing.reshape(groups, capacity * BS, BS), "cube", split_axis=0, concat_axis=0, tiled=True
    )
    arriving = dest_all == own_group
    arriving_i = arriving.astype(jnp.int32)
    rank_ids = jnp.cumsum(arriving_i, axis=1) - arriving_i
    in_position = jnp.where(
        arriving,
        jnp.arange(groups, dtype=jnp.int32)[:, None] * capacity + rank_ids,
        nslots,
    )
    parent_of_slot = (
        jnp.full((nslots,), -1, jnp.int32)
        .at[in_position.reshape(-1)]
        .set(parent_all.reshape(-1), mode="drop")
    )
    assembled = combine_blocks(parent_of_slot, incoming.reshape(nslots, BS, BS), parent_front[0])
    return assembled[None]


def pack_kernel(block_cols, source_ref, update_ref, out_ref):
    def body(slot, carry):
        block = source_ref[slot]
        live = block >= 0
        block = jnp.maximum(block, 0)
        rows = pl.ds(pl.multiple_of((block // block_cols) * BS, BS), BS)
        cols = pl.ds(pl.multiple_of((block % block_cols) * BS, BS), BS)
        out_ref[slot] = jnp.where(live, update_ref[rows, cols], jnp.float32(0.0))
        return carry

    lax.fori_loop(0, out_ref.shape[0], body, 0)


def pack_blocks(source_of_slot, update, block_cols):
    nslots = source_of_slot.shape[0]
    return pl.pallas_call(
        functools.partial(pack_kernel, block_cols),
        out_shape=jax.ShapeDtypeStruct((nslots, BS, BS), update.dtype),
        in_specs=[
            pl.BlockSpec(memory_space=pltpu.SMEM),
            pl.BlockSpec(memory_space=pltpu.VMEM),
        ],
        out_specs=pl.BlockSpec(memory_space=pltpu.VMEM),
    )(source_of_slot, update)


def combine_kernel(parent_ref, incoming_ref, front_ref, out_ref):
    out_ref[...] = front_ref[...]

    def body(slot, carry):
        parent = parent_ref[slot]

        @pl.when(parent >= 0)
        def _():
            cols = pl.ds(pl.multiple_of(parent * BS, BS), BS)
            out_ref[:, cols] = out_ref[:, cols] + incoming_ref[slot]

        return carry

    lax.fori_loop(0, incoming_ref.shape[0], body, 0)


def combine_blocks(parent_of_slot, incoming, front):
    return pl.pallas_call(
        combine_kernel,
        out_shape=jax.ShapeDtypeStruct(front.shape, front.dtype),
        in_specs=[
            pl.BlockSpec(memory_space=pltpu.SMEM),
            pl.BlockSpec(memory_space=pltpu.VMEM),
            pl.BlockSpec(memory_space=pltpu.VMEM),
        ],
        out_specs=pl.BlockSpec(memory_space=pltpu.VMEM),
    )(parent_of_slot, incoming, front)


def factor_kernel(a_ref, inv_ref, work_ref, g_ref):
    n = a_ref.shape[0]
    nb = n // BS
    hp = lax.Precision.HIGHEST
    nt = (((1,), (1,)), ((), ()))
    work_ref[...] = a_ref[...]
    lane = lax.broadcasted_iota(jnp.int32, (1, 2 * BS), 1)
    sub = lax.broadcasted_iota(jnp.int32, (BS, BS), 0)
    col = lax.broadcasted_iota(jnp.int32, (BS, BS), 1)
    eye = (sub == col).astype(jnp.float32)
    diag_inv = []
    rid = lax.broadcasted_iota(jnp.int32, (STRIP, 1), 0)
    for k in range(nb):
        kk = pl.ds(k * BS, BS)
        g_ref[:, :BS] = work_ref[kk, kk]
        g_ref[:, BS:] = eye

        for strip in range(0, BS, STRIP):
            held = g_ref[strip:strip + STRIP, :]
            for local in range(STRIP):
                j = strip + local
                row = held[local:local + 1, :]
                inv_d = 1.0 / jnp.sqrt(row[:, j:j + 1])
                scaled = row * inv_d
                down = jnp.where(rid > local, held[:, j:j + 1] * inv_d, 0.0)
                held = jnp.where(rid == local, scaled, held - down * scaled)
            g_ref[strip:strip + STRIP, :] = held
            below = strip + STRIP
            if below < BS:
                done = g_ref[strip:below, :]
                mult = jnp.transpose(done[:, :BS])[below:, :]
                g_ref[below:, :] = g_ref[below:, :] - jnp.dot(
                    mult, done, precision=hp, preferred_element_type=jnp.float32
                )
        upper = jnp.where(col >= sub, g_ref[:, :BS], 0.0)
        lk_inv = g_ref[:, BS:]
        diag_inv.append(lk_inv)
        work_ref[kk, kk] = jnp.transpose(upper)
        if k < nb - 1:
            rest = pl.ds((k + 1) * BS, n - (k + 1) * BS)
            panel = lax.dot_general(work_ref[rest, kk], lk_inv, nt, precision=hp,
                                    preferred_element_type=jnp.float32)
            work_ref[rest, kk] = panel
            work_ref[rest, rest] = work_ref[rest, rest] - lax.dot_general(
                panel, panel, nt, precision=hp, preferred_element_type=jnp.float32)
    inv_ref[...] = jnp.zeros_like(inv_ref)
    inv_ref[pl.ds(0, BS), pl.ds(0, BS)] = diag_inv[0]
    for i in range(1, nb):
        ii = pl.ds(i * BS, BS)
        left = pl.ds(0, i * BS)
        mixed = jnp.dot(work_ref[ii, left], inv_ref[left, left], precision=hp,
                        preferred_element_type=jnp.float32)
        inv_ref[ii, left] = -jnp.dot(diag_inv[i], mixed, precision=hp,
                                     preferred_element_type=jnp.float32)
        inv_ref[ii, ii] = diag_inv[i]


def factor_inverse(a):
    n = a.shape[0]
    return pl.pallas_call(
        factor_kernel,
        out_shape=jax.ShapeDtypeStruct((n, n), a.dtype),
        in_specs=[pl.BlockSpec(memory_space=pltpu.VMEM)],
        out_specs=pl.BlockSpec(memory_space=pltpu.VMEM),
        scratch_shapes=[pltpu.VMEM((n, n), jnp.float32), pltpu.VMEM((BS, 2 * BS), jnp.float32)],
    )(a)

def solution(mesh):
    placed = (
        P("cube", None, None),
        P("cube", ("row", "col"), None),
        P("cube", "col", "row"),
        P("cube", "col", "row"),
        P("cube"),
        P(None, "col", "row", None, None),
        P(None, "col", "row", None, None),
    )
    return jax.shard_map(
        shards, mesh=mesh, in_specs=placed, out_specs=P("cube", "col", "row"), check_vma=False
    )
```

```python
import functools

import jax
import jax.numpy as jnp
from jax import lax
from jax.experimental import pallas as pl
from jax.experimental.pallas import tpu as pltpu
from jax.sharding import PartitionSpec as P

BS = 128
STRIP = 32


def spread(value, axis, root):
    mine = lax.axis_index(axis) == root
    return lax.psum(jnp.where(mine, value, jnp.zeros_like(value)), axis)


def shards(diag_block, panel, trailing, parent_front, front_order, dest_group, parent_block):
    precise_mode = lax.Precision.HIGHEST
    slab_rows = spread(panel[0], "row", 0)
    col_rows = lax.all_gather(panel[0], "col", axis=0, tiled=True)
    chol_inv = factor_inverse(diag_block[0])
    contract_t = (((1,), (1,)), ((), ()))
    slab_factor = lax.dot_general(slab_rows, chol_inv, contract_t, precision=precise_mode)
    slab_solved = jnp.dot(slab_factor, chol_inv, precision=precise_mode)
    product = lax.dot_general(slab_solved, col_rows, contract_t, precision=precise_mode)
    device_rows = trailing.shape[1]
    cols_dev = trailing.shape[2]
    column_ids = lax.axis_index("row") * cols_dev + jnp.arange(cols_dev, dtype=jnp.int32)
    update = jnp.where(
        column_ids[None, :] < front_order[0], trailing[0] - product, jnp.float32(0.0)
    )
    block_rows = device_rows // BS
    block_cols = cols_dev // BS
    nblocks = block_rows * block_cols
    groups = lax.axis_size("cube")
    own_group = lax.axis_index("cube")
    dest_all = dest_group[:, 0, 0, :, 0]
    parent_all = parent_block[:, 0, 0, :, 0]
    dest_mine = lax.dynamic_index_in_dim(dest_all, own_group, 0, keepdims=False)
    capacity = 2 * nblocks // groups
    nslots = groups * capacity
    hit_table = (dest_mine[:, None] == jnp.arange(groups, dtype=jnp.int32)[None, :]).astype(
        jnp.int32
    )
    before = jnp.cumsum(hit_table, axis=0) - hit_table
    slot_ids = jnp.sum(before * hit_table, axis=1)
    position = dest_mine * capacity + slot_ids
    source_of_slot = (
        jnp.full((nslots,), -1, jnp.int32)
        .at[position]
        .set(jnp.arange(nblocks, dtype=jnp.int32), mode="drop")
    )
    outgoing = pack_blocks(source_of_slot, update, block_cols)
    incoming = lax.all_to_all(
        outgoing.reshape(groups, capacity * BS, BS), "cube", split_axis=0, concat_axis=0, tiled=True
    )
    arriving = dest_all == own_group
    arriving_i = arriving.astype(jnp.int32)
    rank_ids = jnp.cumsum(arriving_i, axis=1) - arriving_i
    in_position = jnp.where(
        arriving,
        jnp.arange(groups, dtype=jnp.int32)[:, None] * capacity + rank_ids,
        nslots,
    )
    parent_of_slot = (
        jnp.full((nslots,), -1, jnp.int32)
        .at[in_position.reshape(-1)]
        .set(parent_all.reshape(-1), mode="drop")
    )
    assembled = combine_blocks(parent_of_slot, incoming.reshape(nslots, BS, BS), parent_front[0])
    return assembled[None]


def pack_kernel(block_cols, source_ref, update_ref, out_ref):
    def body(slot, carry):
        block = source_ref[slot]
        live = block >= 0
        block = jnp.maximum(block, 0)
        rows = pl.ds(pl.multiple_of((block // block_cols) * BS, BS), BS)
        cols = pl.ds(pl.multiple_of((block % block_cols) * BS, BS), BS)
        out_ref[slot] = jnp.where(live, update_ref[rows, cols], jnp.float32(0.0))
        return carry

    lax.fori_loop(0, out_ref.shape[0], body, 0)


def pack_blocks(source_of_slot, update, block_cols):
    nslots = source_of_slot.shape[0]
    return pl.pallas_call(
        functools.partial(pack_kernel, block_cols),
        out_shape=jax.ShapeDtypeStruct((nslots, BS, BS), update.dtype),
        in_specs=[
            pl.BlockSpec(memory_space=pltpu.SMEM),
            pl.BlockSpec(memory_space=pltpu.VMEM),
        ],
        out_specs=pl.BlockSpec(memory_space=pltpu.VMEM),
    )(source_of_slot, update)


def combine_kernel(parent_ref, incoming_ref, front_ref, out_ref):
    out_ref[...] = front_ref[...]

    def body(slot, carry):
        parent = parent_ref[slot]

        @pl.when(parent >= 0)
        def _():
            cols = pl.ds(pl.multiple_of(parent * BS, BS), BS)
            out_ref[:, cols] = out_ref[:, cols] + incoming_ref[slot]

        return carry

    lax.fori_loop(0, incoming_ref.shape[0], body, 0)


def combine_blocks(parent_of_slot, incoming, front):
    return pl.pallas_call(
        combine_kernel,
        out_shape=jax.ShapeDtypeStruct(front.shape, front.dtype),
        in_specs=[
            pl.BlockSpec(memory_space=pltpu.SMEM),
            pl.BlockSpec(memory_space=pltpu.VMEM),
            pl.BlockSpec(memory_space=pltpu.VMEM),
        ],
        out_specs=pl.BlockSpec(memory_space=pltpu.VMEM),
    )(parent_of_slot, incoming, front)


def factor_kernel(a_ref, inv_ref, work_ref, g_ref):
    n = a_ref.shape[0]
    nb = n // BS
    hp = lax.Precision.HIGHEST
    nt = (((1,), (1,)), ((), ()))
    work_ref[...] = a_ref[...]
    lane = lax.broadcasted_iota(jnp.int32, (1, 2 * BS), 1)
    sub = lax.broadcasted_iota(jnp.int32, (BS, BS), 0)
    col = lax.broadcasted_iota(jnp.int32, (BS, BS), 1)
    eye = (sub == col).astype(jnp.float32)
    diag_inv = []
    rid = lax.broadcasted_iota(jnp.int32, (STRIP, 1), 0)
    for k in range(nb):
        kk = pl.ds(k * BS, BS)
        g_ref[:, :BS] = work_ref[kk, kk]
        g_ref[:, BS:] = eye

        for strip in range(0, BS, STRIP):
            held = g_ref[strip:strip + STRIP, :]
            for local in range(STRIP):
                j = strip + local
                row = held[local:local + 1, :]
                factor = jnp.where(rid > local, held[:, j:j + 1] / row[:, j:j + 1], 0.0)
                held = held - factor * row
            pivots = jnp.sum(
                jnp.where(lane[:, :BS] == strip + rid, held[:, :BS], 0.0), axis=1, keepdims=True
            )
            held = held * (1.0 / jnp.sqrt(pivots))
            g_ref[strip:strip + STRIP, :] = held
            below = strip + STRIP
            if below < BS:
                done = g_ref[strip:below, :]
                mult = jnp.transpose(done[:, :BS])[below:, :]
                g_ref[below:, :] = g_ref[below:, :] - jnp.dot(
                    mult, done, precision=hp, preferred_element_type=jnp.float32
                )
        upper = jnp.where(col >= sub, g_ref[:, :BS], 0.0)
        lk_inv = g_ref[:, BS:]
        diag_inv.append(lk_inv)
        work_ref[kk, kk] = jnp.transpose(upper)
        if k < nb - 1:
            rest = pl.ds((k + 1) * BS, n - (k + 1) * BS)
            panel = lax.dot_general(work_ref[rest, kk], lk_inv, nt, precision=hp,
                                    preferred_element_type=jnp.float32)
            work_ref[rest, kk] = panel
            work_ref[rest, rest] = work_ref[rest, rest] - lax.dot_general(
                panel, panel, nt, precision=hp, preferred_element_type=jnp.float32)
    inv_ref[...] = jnp.zeros_like(inv_ref)
    inv_ref[pl.ds(0, BS), pl.ds(0, BS)] = diag_inv[0]
    for i in range(1, nb):
        ii = pl.ds(i * BS, BS)
        left = pl.ds(0, i * BS)
        mixed = jnp.dot(work_ref[ii, left], inv_ref[left, left], precision=hp,
                        preferred_element_type=jnp.float32)
        inv_ref[ii, left] = -jnp.dot(diag_inv[i], mixed, precision=hp,
                                     preferred_element_type=jnp.float32)
        inv_ref[ii, ii] = diag_inv[i]


def factor_inverse(a):
    n = a.shape[0]
    return pl.pallas_call(
        factor_kernel,
        out_shape=jax.ShapeDtypeStruct((n, n), a.dtype),
        in_specs=[pl.BlockSpec(memory_space=pltpu.VMEM)],
        out_specs=pl.BlockSpec(memory_space=pltpu.VMEM),
        scratch_shapes=[pltpu.VMEM((n, n), jnp.float32), pltpu.VMEM((BS, 2 * BS), jnp.float32)],
    )(a)

def solution(mesh):
    placed = (
        P("cube", None, None),
        P("cube", ("row", "col"), None),
        P("cube", "col", "row"),
        P("cube", "col", "row"),
        P("cube"),
        P(None, "col", "row", None, None),
        P(None, "col", "row", None, None),
    )
    return jax.shard_map(
        shards, mesh=mesh, in_specs=placed, out_specs=P("cube", "col", "row"), check_vma=False
    )
```

```python
import functools

import jax
import jax.numpy as jnp
from jax import lax
from jax.experimental import pallas as pl
from jax.experimental.pallas import tpu as pltpu
from jax.sharding import PartitionSpec as P

BS = 128
STRIP = 32


def spread(value, axis, root):
    mine = lax.axis_index(axis) == root
    return lax.psum(jnp.where(mine, value, jnp.zeros_like(value)), axis)


def shards(diag_block, panel, trailing, parent_front, front_order, dest_group, parent_block):
    precise_mode = lax.Precision.HIGHEST
    slab_rows = spread(panel[0], "row", 0)
    col_rows = lax.all_gather(panel[0], "col", axis=0, tiled=True)
    chol_inv = factor_inverse(diag_block[0])
    contract_t = (((1,), (1,)), ((), ()))
    split_mode = lax.Precision.HIGH
    slab_factor = lax.dot_general(slab_rows, chol_inv, contract_t, precision=split_mode)
    slab_solved = jnp.dot(slab_factor, chol_inv, precision=split_mode)
    product = lax.dot_general(slab_solved, col_rows, contract_t, precision=split_mode)
    device_rows = trailing.shape[1]
    cols_dev = trailing.shape[2]
    column_ids = lax.axis_index("row") * cols_dev + jnp.arange(cols_dev, dtype=jnp.int32)
    update = jnp.where(
        column_ids[None, :] < front_order[0], trailing[0] - product, jnp.float32(0.0)
    )
    block_rows = device_rows // BS
    block_cols = cols_dev // BS
    nblocks = block_rows * block_cols
    groups = lax.axis_size("cube")
    own_group = lax.axis_index("cube")
    dest_all = dest_group[:, 0, 0, :, 0]
    parent_all = parent_block[:, 0, 0, :, 0]
    dest_mine = lax.dynamic_index_in_dim(dest_all, own_group, 0, keepdims=False)
    capacity = 2 * nblocks // groups
    nslots = groups * capacity
    hit_table = (dest_mine[:, None] == jnp.arange(groups, dtype=jnp.int32)[None, :]).astype(
        jnp.int32
    )
    before = jnp.cumsum(hit_table, axis=0) - hit_table
    slot_ids = jnp.sum(before * hit_table, axis=1)
    position = dest_mine * capacity + slot_ids
    source_of_slot = (
        jnp.full((nslots,), -1, jnp.int32)
        .at[position]
        .set(jnp.arange(nblocks, dtype=jnp.int32), mode="drop")
    )
    outgoing = pack_blocks(source_of_slot, update, block_cols)
    incoming = lax.all_to_all(
        outgoing.reshape(groups, capacity * BS, BS), "cube", split_axis=0, concat_axis=0, tiled=True
    )
    arriving = dest_all == own_group
    arriving_i = arriving.astype(jnp.int32)
    rank_ids = jnp.cumsum(arriving_i, axis=1) - arriving_i
    in_position = jnp.where(
        arriving,
        jnp.arange(groups, dtype=jnp.int32)[:, None] * capacity + rank_ids,
        nslots,
    )
    parent_of_slot = (
        jnp.full((nslots,), -1, jnp.int32)
        .at[in_position.reshape(-1)]
        .set(parent_all.reshape(-1), mode="drop")
    )
    assembled = combine_blocks(parent_of_slot, incoming.reshape(nslots, BS, BS), parent_front[0])
    return assembled[None]


def pack_kernel(block_cols, source_ref, update_ref, out_ref):
    def body(slot, carry):
        block = source_ref[slot]
        live = block >= 0
        block = jnp.maximum(block, 0)
        rows = pl.ds(pl.multiple_of((block // block_cols) * BS, BS), BS)
        cols = pl.ds(pl.multiple_of((block % block_cols) * BS, BS), BS)
        out_ref[slot] = jnp.where(live, update_ref[rows, cols], jnp.float32(0.0))
        return carry

    lax.fori_loop(0, out_ref.shape[0], body, 0)


def pack_blocks(source_of_slot, update, block_cols):
    nslots = source_of_slot.shape[0]
    return pl.pallas_call(
        functools.partial(pack_kernel, block_cols),
        out_shape=jax.ShapeDtypeStruct((nslots, BS, BS), update.dtype),
        in_specs=[
            pl.BlockSpec(memory_space=pltpu.SMEM),
            pl.BlockSpec(memory_space=pltpu.VMEM),
        ],
        out_specs=pl.BlockSpec(memory_space=pltpu.VMEM),
    )(source_of_slot, update)


def combine_kernel(parent_ref, incoming_ref, front_ref, out_ref):
    out_ref[...] = front_ref[...]

    def body(slot, carry):
        parent = parent_ref[slot]

        @pl.when(parent >= 0)
        def _():
            cols = pl.ds(pl.multiple_of(parent * BS, BS), BS)
            out_ref[:, cols] = out_ref[:, cols] + incoming_ref[slot]

        return carry

    lax.fori_loop(0, incoming_ref.shape[0], body, 0)


def combine_blocks(parent_of_slot, incoming, front):
    return pl.pallas_call(
        combine_kernel,
        out_shape=jax.ShapeDtypeStruct(front.shape, front.dtype),
        in_specs=[
            pl.BlockSpec(memory_space=pltpu.SMEM),
            pl.BlockSpec(memory_space=pltpu.VMEM),
            pl.BlockSpec(memory_space=pltpu.VMEM),
        ],
        out_specs=pl.BlockSpec(memory_space=pltpu.VMEM),
    )(parent_of_slot, incoming, front)


def factor_kernel(a_ref, inv_ref, work_ref, g_ref):
    n = a_ref.shape[0]
    nb = n // BS
    hp = lax.Precision.HIGHEST
    nt = (((1,), (1,)), ((), ()))
    work_ref[...] = a_ref[...]
    lane = lax.broadcasted_iota(jnp.int32, (1, 2 * BS), 1)
    sub = lax.broadcasted_iota(jnp.int32, (BS, BS), 0)
    col = lax.broadcasted_iota(jnp.int32, (BS, BS), 1)
    eye = (sub == col).astype(jnp.float32)
    diag_inv = []
    rid = lax.broadcasted_iota(jnp.int32, (STRIP, 1), 0)
    for k in range(nb):
        kk = pl.ds(k * BS, BS)
        g_ref[:, :BS] = work_ref[kk, kk]
        g_ref[:, BS:] = eye

        for strip in range(0, BS, STRIP):
            held = g_ref[strip:strip + STRIP, :]
            for local in range(STRIP):
                j = strip + local
                row = held[local:local + 1, :]
                factor = jnp.where(rid > local, held[:, j:j + 1] / row[:, j:j + 1], 0.0)
                held = held - factor * row
            pivots = jnp.sum(
                jnp.where(lane[:, :BS] == strip + rid, held[:, :BS], 0.0), axis=1, keepdims=True
            )
            held = held * (1.0 / jnp.sqrt(pivots))
            g_ref[strip:strip + STRIP, :] = held
            below = strip + STRIP
            if below < BS:
                done = g_ref[strip:below, :]
                mult = jnp.transpose(done[:, :BS])[below:, :]
                g_ref[below:, :] = g_ref[below:, :] - jnp.dot(
                    mult, done, precision=hp, preferred_element_type=jnp.float32
                )
        upper = jnp.where(col >= sub, g_ref[:, :BS], 0.0)
        lk_inv = g_ref[:, BS:]
        diag_inv.append(lk_inv)
        work_ref[kk, kk] = jnp.transpose(upper)
        if k < nb - 1:
            rest = pl.ds((k + 1) * BS, n - (k + 1) * BS)
            panel = lax.dot_general(work_ref[rest, kk], lk_inv, nt, precision=hp,
                                    preferred_element_type=jnp.float32)
            work_ref[rest, kk] = panel
            work_ref[rest, rest] = work_ref[rest, rest] - lax.dot_general(
                panel, panel, nt, precision=hp, preferred_element_type=jnp.float32)
    inv_ref[...] = jnp.zeros_like(inv_ref)
    inv_ref[pl.ds(0, BS), pl.ds(0, BS)] = diag_inv[0]
    for i in range(1, nb):
        ii = pl.ds(i * BS, BS)
        left = pl.ds(0, i * BS)
        mixed = jnp.dot(work_ref[ii, left], inv_ref[left, left], precision=hp,
                        preferred_element_type=jnp.float32)
        inv_ref[ii, left] = -jnp.dot(diag_inv[i], mixed, precision=hp,
                                     preferred_element_type=jnp.float32)
        inv_ref[ii, ii] = diag_inv[i]


def factor_inverse(a):
    n = a.shape[0]
    return pl.pallas_call(
        factor_kernel,
        out_shape=jax.ShapeDtypeStruct((n, n), a.dtype),
        in_specs=[pl.BlockSpec(memory_space=pltpu.VMEM)],
        out_specs=pl.BlockSpec(memory_space=pltpu.VMEM),
        scratch_shapes=[pltpu.VMEM((n, n), jnp.float32), pltpu.VMEM((BS, 2 * BS), jnp.float32)],
    )(a)

def solution(mesh):
    placed = (
        P("cube", None, None),
        P("cube", ("row", "col"), None),
        P("cube", "col", "row"),
        P("cube", "col", "row"),
        P("cube"),
        P(None, "col", "row", None, None),
        P(None, "col", "row", None, None),
    )
    return jax.shard_map(
        shards, mesh=mesh, in_specs=placed, out_specs=P("cube", "col", "row"), check_vma=False
    )
```

```python
import functools

import jax
import jax.numpy as jnp
from jax import lax
from jax.experimental import pallas as pl
from jax.experimental.pallas import tpu as pltpu
from jax.sharding import PartitionSpec as P

BS = 128
STRIP = 32


def spread(value, axis, root):
    mine = lax.axis_index(axis) == root
    return lax.psum(jnp.where(mine, value, jnp.zeros_like(value)), axis)


def shards(diag_block, panel, trailing, parent_front, front_order, dest_group, parent_block):
    precise_mode = lax.Precision.HIGHEST
    slab_rows = spread(panel[0], "row", 0)
    col_rows = lax.all_gather(panel[0], "col", axis=0, tiled=True)
    chol_inv = factor_inverse(diag_block[0])
    contract_t = (((1,), (1,)), ((), ()))
    split_mode = lax.Precision.HIGH
    slab_factor = lax.dot_general(slab_rows, chol_inv, contract_t, precision=split_mode)
    slab_solved = jnp.dot(slab_factor, chol_inv, precision=split_mode)
    product = lax.dot_general(slab_solved, col_rows, contract_t, precision=split_mode)
    device_rows = trailing.shape[1]
    cols_dev = trailing.shape[2]
    column_ids = lax.axis_index("row") * cols_dev + jnp.arange(cols_dev, dtype=jnp.int32)
    update = jnp.where(
        column_ids[None, :] < front_order[0], trailing[0] - product, jnp.float32(0.0)
    )
    block_rows = device_rows // BS
    block_cols = cols_dev // BS
    nblocks = block_rows * block_cols
    groups = lax.axis_size("cube")
    own_group = lax.axis_index("cube")
    dest_all = dest_group[:, 0, 0, :, 0]
    parent_all = parent_block[:, 0, 0, :, 0]
    dest_mine = lax.dynamic_index_in_dim(dest_all, own_group, 0, keepdims=False)
    capacity = 2 * nblocks // groups
    nslots = groups * capacity
    hit_table = (dest_mine[:, None] == jnp.arange(groups, dtype=jnp.int32)[None, :]).astype(
        jnp.int32
    )
    before = jnp.cumsum(hit_table, axis=0) - hit_table
    slot_ids = jnp.sum(before * hit_table, axis=1)
    position = dest_mine * capacity + slot_ids
    source_of_slot = (
        jnp.full((nslots,), -1, jnp.int32)
        .at[position]
        .set(jnp.arange(nblocks, dtype=jnp.int32), mode="drop")
    )
    outgoing = pack_blocks(source_of_slot, update, block_cols)
    incoming = lax.all_to_all(
        outgoing.reshape(groups, capacity * BS, BS), "cube", split_axis=0, concat_axis=0, tiled=True
    )
    arriving = dest_all == own_group
    arriving_i = arriving.astype(jnp.int32)
    rank_ids = jnp.cumsum(arriving_i, axis=1) - arriving_i
    in_position = jnp.where(
        arriving,
        jnp.arange(groups, dtype=jnp.int32)[:, None] * capacity + rank_ids,
        nslots,
    )
    parent_of_slot = (
        jnp.full((nslots,), -1, jnp.int32)
        .at[in_position.reshape(-1)]
        .set(parent_all.reshape(-1), mode="drop")
    )
    assembled = combine_blocks(parent_of_slot, incoming.reshape(nslots, BS, BS), parent_front[0])
    return assembled[None]


def pack_kernel(block_cols, source_ref, update_ref, out_ref, sems):
    nslots = out_ref.shape[0]

    def start(slot, carry):
        block = source_ref[slot]

        @pl.when(block >= 0)
        def _():
            rows = pl.ds(pl.multiple_of((block // block_cols) * BS, BS), BS)
            cols = pl.ds(pl.multiple_of((block % block_cols) * BS, BS), BS)
            pltpu.make_async_copy(update_ref.at[rows, cols], out_ref.at[slot], sems.at[slot]).start()

        return carry

    def finish(slot, carry):
        block = source_ref[slot]

        @pl.when(block >= 0)
        def _():
            pltpu.make_async_copy(
                update_ref.at[pl.ds(0, BS), pl.ds(0, BS)], out_ref.at[slot], sems.at[slot]
            ).wait()

        return carry

    lax.fori_loop(0, nslots, start, 0)
    lax.fori_loop(0, nslots, finish, 0)


def pack_blocks(source_of_slot, update, block_cols):
    nslots = source_of_slot.shape[0]
    return pl.pallas_call(
        functools.partial(pack_kernel, block_cols),
        out_shape=jax.ShapeDtypeStruct((nslots, BS, BS), update.dtype),
        in_specs=[
            pl.BlockSpec(memory_space=pltpu.SMEM),
            pl.BlockSpec(memory_space=pltpu.VMEM),
        ],
        out_specs=pl.BlockSpec(memory_space=pl.ANY),
        scratch_shapes=[pltpu.SemaphoreType.DMA((nslots,))],
    )(source_of_slot, update)


def combine_kernel(parent_ref, incoming_ref, front_ref, out_ref):
    out_ref[...] = front_ref[...]

    def body(slot, carry):
        parent = parent_ref[slot]

        @pl.when(parent >= 0)
        def _():
            cols = pl.ds(pl.multiple_of(parent * BS, BS), BS)
            out_ref[:, cols] = out_ref[:, cols] + incoming_ref[slot]

        return carry

    lax.fori_loop(0, incoming_ref.shape[0], body, 0)


def combine_blocks(parent_of_slot, incoming, front):
    return pl.pallas_call(
        combine_kernel,
        out_shape=jax.ShapeDtypeStruct(front.shape, front.dtype),
        in_specs=[
            pl.BlockSpec(memory_space=pltpu.SMEM),
            pl.BlockSpec(memory_space=pltpu.VMEM),
            pl.BlockSpec(memory_space=pltpu.VMEM),
        ],
        out_specs=pl.BlockSpec(memory_space=pltpu.VMEM),
    )(parent_of_slot, incoming, front)


def factor_kernel(a_ref, inv_ref, work_ref, g_ref):
    n = a_ref.shape[0]
    nb = n // BS
    hp = lax.Precision.HIGHEST
    nt = (((1,), (1,)), ((), ()))
    work_ref[...] = a_ref[...]
    lane = lax.broadcasted_iota(jnp.int32, (1, 2 * BS), 1)
    sub = lax.broadcasted_iota(jnp.int32, (BS, BS), 0)
    col = lax.broadcasted_iota(jnp.int32, (BS, BS), 1)
    eye = (sub == col).astype(jnp.float32)
    diag_inv = []
    rid = lax.broadcasted_iota(jnp.int32, (STRIP, 1), 0)
    for k in range(nb):
        kk = pl.ds(k * BS, BS)
        g_ref[:, :BS] = work_ref[kk, kk]
        g_ref[:, BS:] = eye

        for strip in range(0, BS, STRIP):
            held = g_ref[strip:strip + STRIP, :]
            for local in range(STRIP):
                j = strip + local
                row = held[local:local + 1, :]
                factor = jnp.where(rid > local, held[:, j:j + 1] / row[:, j:j + 1], 0.0)
                held = held - factor * row
            pivots = jnp.sum(
                jnp.where(lane[:, :BS] == strip + rid, held[:, :BS], 0.0), axis=1, keepdims=True
            )
            held = held * (1.0 / jnp.sqrt(pivots))
            g_ref[strip:strip + STRIP, :] = held
            below = strip + STRIP
            if below < BS:
                done = g_ref[strip:below, :]
                mult = jnp.transpose(done[:, :BS])[below:, :]
                g_ref[below:, :] = g_ref[below:, :] - jnp.dot(
                    mult, done, precision=hp, preferred_element_type=jnp.float32
                )
        upper = jnp.where(col >= sub, g_ref[:, :BS], 0.0)
        lk_inv = g_ref[:, BS:]
        diag_inv.append(lk_inv)
        work_ref[kk, kk] = jnp.transpose(upper)
        if k < nb - 1:
            rest = pl.ds((k + 1) * BS, n - (k + 1) * BS)
            panel = lax.dot_general(work_ref[rest, kk], lk_inv, nt, precision=hp,
                                    preferred_element_type=jnp.float32)
            work_ref[rest, kk] = panel
            work_ref[rest, rest] = work_ref[rest, rest] - lax.dot_general(
                panel, panel, nt, precision=hp, preferred_element_type=jnp.float32)
    inv_ref[...] = jnp.zeros_like(inv_ref)
    inv_ref[pl.ds(0, BS), pl.ds(0, BS)] = diag_inv[0]
    for i in range(1, nb):
        ii = pl.ds(i * BS, BS)
        left = pl.ds(0, i * BS)
        mixed = jnp.dot(work_ref[ii, left], inv_ref[left, left], precision=hp,
                        preferred_element_type=jnp.float32)
        inv_ref[ii, left] = -jnp.dot(diag_inv[i], mixed, precision=hp,
                                     preferred_element_type=jnp.float32)
        inv_ref[ii, ii] = diag_inv[i]


def factor_inverse(a):
    n = a.shape[0]
    return pl.pallas_call(
        factor_kernel,
        out_shape=jax.ShapeDtypeStruct((n, n), a.dtype),
        in_specs=[pl.BlockSpec(memory_space=pltpu.VMEM)],
        out_specs=pl.BlockSpec(memory_space=pltpu.VMEM),
        scratch_shapes=[pltpu.VMEM((n, n), jnp.float32), pltpu.VMEM((BS, 2 * BS), jnp.float32)],
    )(a)

def solution(mesh):
    placed = (
        P("cube", None, None),
        P("cube", ("row", "col"), None),
        P("cube", "col", "row"),
        P("cube", "col", "row"),
        P("cube"),
        P(None, "col", "row", None, None),
        P(None, "col", "row", None, None),
    )
    return jax.shard_map(
        shards, mesh=mesh, in_specs=placed, out_specs=P("cube", "col", "row"), check_vma=False
    )
```

```python
import functools

import jax
import jax.numpy as jnp
from jax import lax
from jax.experimental import pallas as pl
from jax.experimental.pallas import tpu as pltpu
from jax.sharding import PartitionSpec as P

BS = 128
STRIP = 32


def spread(value, axis, root):
    mine = lax.axis_index(axis) == root
    return lax.psum(jnp.where(mine, value, jnp.zeros_like(value)), axis)


def shards(diag_block, panel, trailing, parent_front, front_order, dest_group, parent_block):
    precise_mode = lax.Precision.HIGHEST
    slab_rows = spread(panel[0], "row", 0)
    col_rows = lax.all_gather(panel[0], "col", axis=0, tiled=True)
    chol_inv = factor_inverse(diag_block[0])
    contract_t = (((1,), (1,)), ((), ()))
    split_mode = lax.Precision.HIGH
    slab_factor = lax.dot_general(slab_rows, chol_inv, contract_t, precision=split_mode)
    slab_solved = jnp.dot(slab_factor, chol_inv, precision=split_mode)
    product = lax.dot_general(slab_solved, col_rows, contract_t, precision=split_mode)
    device_rows = trailing.shape[1]
    cols_dev = trailing.shape[2]
    column_ids = lax.axis_index("row") * cols_dev + jnp.arange(cols_dev, dtype=jnp.int32)
    update = jnp.where(
        column_ids[None, :] < front_order[0], trailing[0] - product, jnp.float32(0.0)
    )
    block_rows = device_rows // BS
    block_cols = cols_dev // BS
    nblocks = block_rows * block_cols
    groups = lax.axis_size("cube")
    own_group = lax.axis_index("cube")
    dest_all = dest_group[:, 0, 0, :, 0]
    parent_all = parent_block[:, 0, 0, :, 0]
    dest_mine = lax.dynamic_index_in_dim(dest_all, own_group, 0, keepdims=False)
    capacity = 2 * nblocks // groups
    nslots = groups * capacity
    hit_table = (dest_mine[:, None] == jnp.arange(groups, dtype=jnp.int32)[None, :]).astype(
        jnp.int32
    )
    before = jnp.cumsum(hit_table, axis=0) - hit_table
    slot_ids = jnp.sum(before * hit_table, axis=1)
    position = dest_mine * capacity + slot_ids
    source_of_slot = (
        jnp.full((nslots,), -1, jnp.int32)
        .at[position]
        .set(jnp.arange(nblocks, dtype=jnp.int32), mode="drop")
    )
    outgoing = pack_blocks(source_of_slot, update, block_cols)
    incoming = lax.all_to_all(
        outgoing.reshape(groups, capacity * BS, BS), "cube", split_axis=0, concat_axis=0, tiled=True
    )
    arriving = dest_all == own_group
    arriving_i = arriving.astype(jnp.int32)
    rank_ids = jnp.cumsum(arriving_i, axis=1) - arriving_i
    in_position = jnp.where(
        arriving,
        jnp.arange(groups, dtype=jnp.int32)[:, None] * capacity + rank_ids,
        nslots,
    )
    parent_of_slot = (
        jnp.full((nslots,), -1, jnp.int32)
        .at[in_position.reshape(-1)]
        .set(parent_all.reshape(-1), mode="drop")
    )
    assembled = combine_blocks(parent_of_slot, incoming.reshape(nslots, BS, BS), parent_front[0])
    return assembled[None]


def pack_kernel(block_cols, source_ref, update_ref, out_ref, sems):
    nslots = out_ref.shape[0]

    def start(slot, carry):
        block = source_ref[slot]

        @pl.when(block >= 0)
        def _():
            rows = pl.ds(pl.multiple_of((block // block_cols) * BS, BS), BS)
            cols = pl.ds(pl.multiple_of((block % block_cols) * BS, BS), BS)
            pltpu.make_async_copy(update_ref.at[rows, cols], out_ref.at[slot], sems.at[slot]).start()

        return carry

    def finish(slot, carry):
        block = source_ref[slot]

        @pl.when(block >= 0)
        def _():
            pltpu.make_async_copy(
                update_ref.at[pl.ds(0, BS), pl.ds(0, BS)], out_ref.at[slot], sems.at[slot]
            ).wait()

        return carry

    lax.fori_loop(0, nslots, start, 0)
    lax.fori_loop(0, nslots, finish, 0)


def pack_blocks(source_of_slot, update, block_cols):
    nslots = source_of_slot.shape[0]
    return pl.pallas_call(
        functools.partial(pack_kernel, block_cols),
        out_shape=jax.ShapeDtypeStruct((nslots, BS, BS), update.dtype),
        in_specs=[
            pl.BlockSpec(memory_space=pltpu.SMEM),
            pl.BlockSpec(memory_space=pltpu.VMEM),
        ],
        out_specs=pl.BlockSpec(memory_space=pl.ANY),
        scratch_shapes=[pltpu.SemaphoreType.DMA((nslots,))],
    )(source_of_slot, update)


def combine_kernel(parent_ref, incoming_ref, front_ref, out_ref, landed, sems):
    nslots = incoming_ref.shape[0]

    def start(slot, carry):
        @pl.when(parent_ref[slot] >= 0)
        def _():
            pltpu.make_async_copy(incoming_ref.at[slot], landed.at[slot], sems.at[slot]).start()

        return carry

    lax.fori_loop(0, nslots, start, 0)
    out_ref[...] = front_ref[...]

    def body(slot, carry):
        parent = parent_ref[slot]

        @pl.when(parent >= 0)
        def _():
            pltpu.make_async_copy(incoming_ref.at[slot], landed.at[slot], sems.at[slot]).wait()
            cols = pl.ds(pl.multiple_of(parent * BS, BS), BS)
            out_ref[:, cols] = out_ref[:, cols] + landed[slot]

        return carry

    lax.fori_loop(0, nslots, body, 0)


def combine_blocks(parent_of_slot, incoming, front):
    nslots = incoming.shape[0]
    return pl.pallas_call(
        combine_kernel,
        out_shape=jax.ShapeDtypeStruct(front.shape, front.dtype),
        in_specs=[
            pl.BlockSpec(memory_space=pltpu.SMEM),
            pl.BlockSpec(memory_space=pl.ANY),
            pl.BlockSpec(memory_space=pltpu.VMEM),
        ],
        out_specs=pl.BlockSpec(memory_space=pltpu.VMEM),
        scratch_shapes=[
            pltpu.VMEM((nslots, BS, BS), incoming.dtype),
            pltpu.SemaphoreType.DMA((nslots,)),
        ],
    )(parent_of_slot, incoming, front)


def factor_kernel(a_ref, inv_ref, work_ref, g_ref):
    n = a_ref.shape[0]
    nb = n // BS
    hp = lax.Precision.HIGHEST
    nt = (((1,), (1,)), ((), ()))
    work_ref[...] = a_ref[...]
    lane = lax.broadcasted_iota(jnp.int32, (1, 2 * BS), 1)
    sub = lax.broadcasted_iota(jnp.int32, (BS, BS), 0)
    col = lax.broadcasted_iota(jnp.int32, (BS, BS), 1)
    eye = (sub == col).astype(jnp.float32)
    diag_inv = []
    rid = lax.broadcasted_iota(jnp.int32, (STRIP, 1), 0)
    for k in range(nb):
        kk = pl.ds(k * BS, BS)
        g_ref[:, :BS] = work_ref[kk, kk]
        g_ref[:, BS:] = eye

        for strip in range(0, BS, STRIP):
            held = g_ref[strip:strip + STRIP, :]
            for local in range(STRIP):
                j = strip + local
                row = held[local:local + 1, :]
                factor = jnp.where(rid > local, held[:, j:j + 1] / row[:, j:j + 1], 0.0)
                held = held - factor * row
            pivots = jnp.sum(
                jnp.where(lane[:, :BS] == strip + rid, held[:, :BS], 0.0), axis=1, keepdims=True
            )
            held = held * (1.0 / jnp.sqrt(pivots))
            g_ref[strip:strip + STRIP, :] = held
            below = strip + STRIP
            if below < BS:
                done = g_ref[strip:below, :]
                mult = jnp.transpose(done[:, :BS])[below:, :]
                g_ref[below:, :] = g_ref[below:, :] - jnp.dot(
                    mult, done, precision=hp, preferred_element_type=jnp.float32
                )
        upper = jnp.where(col >= sub, g_ref[:, :BS], 0.0)
        lk_inv = g_ref[:, BS:]
        diag_inv.append(lk_inv)
        work_ref[kk, kk] = jnp.transpose(upper)
        if k < nb - 1:
            rest = pl.ds((k + 1) * BS, n - (k + 1) * BS)
            panel = lax.dot_general(work_ref[rest, kk], lk_inv, nt, precision=hp,
                                    preferred_element_type=jnp.float32)
            work_ref[rest, kk] = panel
            work_ref[rest, rest] = work_ref[rest, rest] - lax.dot_general(
                panel, panel, nt, precision=hp, preferred_element_type=jnp.float32)
    inv_ref[...] = jnp.zeros_like(inv_ref)
    inv_ref[pl.ds(0, BS), pl.ds(0, BS)] = diag_inv[0]
    for i in range(1, nb):
        ii = pl.ds(i * BS, BS)
        left = pl.ds(0, i * BS)
        mixed = jnp.dot(work_ref[ii, left], inv_ref[left, left], precision=hp,
                        preferred_element_type=jnp.float32)
        inv_ref[ii, left] = -jnp.dot(diag_inv[i], mixed, precision=hp,
                                     preferred_element_type=jnp.float32)
        inv_ref[ii, ii] = diag_inv[i]


def factor_inverse(a):
    n = a.shape[0]
    return pl.pallas_call(
        factor_kernel,
        out_shape=jax.ShapeDtypeStruct((n, n), a.dtype),
        in_specs=[pl.BlockSpec(memory_space=pltpu.VMEM)],
        out_specs=pl.BlockSpec(memory_space=pltpu.VMEM),
        scratch_shapes=[pltpu.VMEM((n, n), jnp.float32), pltpu.VMEM((BS, 2 * BS), jnp.float32)],
    )(a)

def solution(mesh):
    placed = (
        P("cube", None, None),
        P("cube", ("row", "col"), None),
        P("cube", "col", "row"),
        P("cube", "col", "row"),
        P("cube"),
        P(None, "col", "row", None, None),
        P(None, "col", "row", None, None),
    )
    return jax.shard_map(
        shards, mesh=mesh, in_specs=placed, out_specs=P("cube", "col", "row"), check_vma=False
    )
```

```python
import functools

import jax
import jax.numpy as jnp
from jax import lax
from jax.experimental import pallas as pl
from jax.experimental.pallas import tpu as pltpu
from jax.sharding import PartitionSpec as P

BS = 128
STRIP = 32


def spread(value, axis, root):
    mine = lax.axis_index(axis) == root
    return lax.psum(jnp.where(mine, value, jnp.zeros_like(value)), axis)


def shards(diag_block, panel, trailing, parent_front, front_order, dest_group, parent_block):
    precise_mode = lax.Precision.HIGHEST
    slab_rows = lax.all_gather(panel[0], "row", axis=0, tiled=True)[: panel.shape[1]]
    col_rows = lax.all_gather(panel[0], "col", axis=0, tiled=True)
    chol_inv = factor_inverse(diag_block[0])
    contract_t = (((1,), (1,)), ((), ()))
    split_mode = lax.Precision.HIGH
    slab_factor = lax.dot_general(slab_rows, chol_inv, contract_t, precision=split_mode)
    slab_solved = jnp.dot(slab_factor, chol_inv, precision=split_mode)
    product = lax.dot_general(slab_solved, col_rows, contract_t, precision=split_mode)
    device_rows = trailing.shape[1]
    cols_dev = trailing.shape[2]
    column_ids = lax.axis_index("row") * cols_dev + jnp.arange(cols_dev, dtype=jnp.int32)
    update = jnp.where(
        column_ids[None, :] < front_order[0], trailing[0] - product, jnp.float32(0.0)
    )
    block_rows = device_rows // BS
    block_cols = cols_dev // BS
    nblocks = block_rows * block_cols
    groups = lax.axis_size("cube")
    own_group = lax.axis_index("cube")
    dest_all = dest_group[:, 0, 0, :, 0]
    parent_all = parent_block[:, 0, 0, :, 0]
    dest_mine = lax.dynamic_index_in_dim(dest_all, own_group, 0, keepdims=False)
    capacity = 2 * nblocks // groups
    nslots = groups * capacity
    hit_table = (dest_mine[:, None] == jnp.arange(groups, dtype=jnp.int32)[None, :]).astype(
        jnp.int32
    )
    before = jnp.cumsum(hit_table, axis=0) - hit_table
    slot_ids = jnp.sum(before * hit_table, axis=1)
    position = dest_mine * capacity + slot_ids
    source_of_slot = (
        jnp.full((nslots,), -1, jnp.int32)
        .at[position]
        .set(jnp.arange(nblocks, dtype=jnp.int32), mode="drop")
    )
    outgoing = pack_blocks(source_of_slot, update, block_cols)
    incoming = lax.all_to_all(
        outgoing.reshape(groups, capacity * BS, BS), "cube", split_axis=0, concat_axis=0, tiled=True
    )
    arriving = dest_all == own_group
    arriving_i = arriving.astype(jnp.int32)
    rank_ids = jnp.cumsum(arriving_i, axis=1) - arriving_i
    in_position = jnp.where(
        arriving,
        jnp.arange(groups, dtype=jnp.int32)[:, None] * capacity + rank_ids,
        nslots,
    )
    parent_of_slot = (
        jnp.full((nslots,), -1, jnp.int32)
        .at[in_position.reshape(-1)]
        .set(parent_all.reshape(-1), mode="drop")
    )
    assembled = combine_blocks(parent_of_slot, incoming.reshape(nslots, BS, BS), parent_front[0])
    return assembled[None]


def pack_kernel(block_cols, source_ref, update_ref, out_ref, sems):
    nslots = out_ref.shape[0]

    def start(slot, carry):
        block = source_ref[slot]

        @pl.when(block >= 0)
        def _():
            rows = pl.ds(pl.multiple_of((block // block_cols) * BS, BS), BS)
            cols = pl.ds(pl.multiple_of((block % block_cols) * BS, BS), BS)
            pltpu.make_async_copy(update_ref.at[rows, cols], out_ref.at[slot], sems.at[slot]).start()

        return carry

    def finish(slot, carry):
        block = source_ref[slot]

        @pl.when(block >= 0)
        def _():
            pltpu.make_async_copy(
                update_ref.at[pl.ds(0, BS), pl.ds(0, BS)], out_ref.at[slot], sems.at[slot]
            ).wait()

        return carry

    lax.fori_loop(0, nslots, start, 0)
    lax.fori_loop(0, nslots, finish, 0)


def pack_blocks(source_of_slot, update, block_cols):
    nslots = source_of_slot.shape[0]
    return pl.pallas_call(
        functools.partial(pack_kernel, block_cols),
        out_shape=jax.ShapeDtypeStruct((nslots, BS, BS), update.dtype),
        in_specs=[
            pl.BlockSpec(memory_space=pltpu.SMEM),
            pl.BlockSpec(memory_space=pltpu.VMEM),
        ],
        out_specs=pl.BlockSpec(memory_space=pl.ANY),
        scratch_shapes=[pltpu.SemaphoreType.DMA((nslots,))],
    )(source_of_slot, update)


def combine_kernel(parent_ref, incoming_ref, front_ref, out_ref):
    out_ref[...] = front_ref[...]

    def body(slot, carry):
        parent = parent_ref[slot]

        @pl.when(parent >= 0)
        def _():
            cols = pl.ds(pl.multiple_of(parent * BS, BS), BS)
            out_ref[:, cols] = out_ref[:, cols] + incoming_ref[slot]

        return carry

    lax.fori_loop(0, incoming_ref.shape[0], body, 0)


def combine_blocks(parent_of_slot, incoming, front):
    return pl.pallas_call(
        combine_kernel,
        out_shape=jax.ShapeDtypeStruct(front.shape, front.dtype),
        in_specs=[
            pl.BlockSpec(memory_space=pltpu.SMEM),
            pl.BlockSpec(memory_space=pltpu.VMEM),
            pl.BlockSpec(memory_space=pltpu.VMEM),
        ],
        out_specs=pl.BlockSpec(memory_space=pltpu.VMEM),
    )(parent_of_slot, incoming, front)


def factor_kernel(a_ref, inv_ref, work_ref, g_ref):
    n = a_ref.shape[0]
    nb = n // BS
    hp = lax.Precision.HIGHEST
    nt = (((1,), (1,)), ((), ()))
    work_ref[...] = a_ref[...]
    lane = lax.broadcasted_iota(jnp.int32, (1, 2 * BS), 1)
    sub = lax.broadcasted_iota(jnp.int32, (BS, BS), 0)
    col = lax.broadcasted_iota(jnp.int32, (BS, BS), 1)
    eye = (sub == col).astype(jnp.float32)
    diag_inv = []
    rid = lax.broadcasted_iota(jnp.int32, (STRIP, 1), 0)
    for k in range(nb):
        kk = pl.ds(k * BS, BS)
        g_ref[:, :BS] = work_ref[kk, kk]
        g_ref[:, BS:] = eye

        for strip in range(0, BS, STRIP):
            held = g_ref[strip:strip + STRIP, :]
            for local in range(STRIP):
                j = strip + local
                row = held[local:local + 1, :]
                factor = jnp.where(rid > local, held[:, j:j + 1] / row[:, j:j + 1], 0.0)
                held = held - factor * row
            pivots = jnp.sum(
                jnp.where(lane[:, :BS] == strip + rid, held[:, :BS], 0.0), axis=1, keepdims=True
            )
            held = held * (1.0 / jnp.sqrt(pivots))
            g_ref[strip:strip + STRIP, :] = held
            below = strip + STRIP
            if below < BS:
                done = g_ref[strip:below, :]
                mult = jnp.transpose(done[:, :BS])[below:, :]
                g_ref[below:, :] = g_ref[below:, :] - jnp.dot(
                    mult, done, precision=hp, preferred_element_type=jnp.float32
                )
        upper = jnp.where(col >= sub, g_ref[:, :BS], 0.0)
        lk_inv = g_ref[:, BS:]
        diag_inv.append(lk_inv)
        work_ref[kk, kk] = jnp.transpose(upper)
        if k < nb - 1:
            rest = pl.ds((k + 1) * BS, n - (k + 1) * BS)
            panel = lax.dot_general(work_ref[rest, kk], lk_inv, nt, precision=hp,
                                    preferred_element_type=jnp.float32)
            work_ref[rest, kk] = panel
            work_ref[rest, rest] = work_ref[rest, rest] - lax.dot_general(
                panel, panel, nt, precision=hp, preferred_element_type=jnp.float32)
    inv_ref[...] = jnp.zeros_like(inv_ref)
    inv_ref[pl.ds(0, BS), pl.ds(0, BS)] = diag_inv[0]
    for i in range(1, nb):
        ii = pl.ds(i * BS, BS)
        left = pl.ds(0, i * BS)
        mixed = jnp.dot(work_ref[ii, left], inv_ref[left, left], precision=hp,
                        preferred_element_type=jnp.float32)
        inv_ref[ii, left] = -jnp.dot(diag_inv[i], mixed, precision=hp,
                                     preferred_element_type=jnp.float32)
        inv_ref[ii, ii] = diag_inv[i]


def factor_inverse(a):
    n = a.shape[0]
    return pl.pallas_call(
        factor_kernel,
        out_shape=jax.ShapeDtypeStruct((n, n), a.dtype),
        in_specs=[pl.BlockSpec(memory_space=pltpu.VMEM)],
        out_specs=pl.BlockSpec(memory_space=pltpu.VMEM),
        scratch_shapes=[pltpu.VMEM((n, n), jnp.float32), pltpu.VMEM((BS, 2 * BS), jnp.float32)],
    )(a)

def solution(mesh):
    placed = (
        P("cube", None, None),
        P("cube", ("row", "col"), None),
        P("cube", "col", "row"),
        P("cube", "col", "row"),
        P("cube"),
        P(None, "col", "row", None, None),
        P(None, "col", "row", None, None),
    )
    return jax.shard_map(
        shards, mesh=mesh, in_specs=placed, out_specs=P("cube", "col", "row"), check_vma=False
    )
```

```python
import functools

import jax
import jax.numpy as jnp
from jax import lax
from jax.experimental import pallas as pl
from jax.experimental.pallas import tpu as pltpu
from jax.sharding import PartitionSpec as P

BS = 128
STRIP = 32


def spread(value, axis, root):
    count = lax.axis_size(axis)
    received = [lax.ppermute(value, axis, [(root, k)]) for k in range(count) if k != root]
    mine = lax.axis_index(axis) == root
    return jnp.where(mine, value, sum(received[1:], received[0]))


def shards(diag_block, panel, trailing, parent_front, front_order, dest_group, parent_block):
    precise_mode = lax.Precision.HIGHEST
    slab_rows = spread(panel[0], "row", 0)
    col_rows = lax.all_gather(panel[0], "col", axis=0, tiled=True)
    chol_inv = factor_inverse(diag_block[0])
    contract_t = (((1,), (1,)), ((), ()))
    split_mode = lax.Precision.HIGH
    slab_factor = lax.dot_general(slab_rows, chol_inv, contract_t, precision=split_mode)
    slab_solved = jnp.dot(slab_factor, chol_inv, precision=split_mode)
    product = lax.dot_general(slab_solved, col_rows, contract_t, precision=split_mode)
    device_rows = trailing.shape[1]
    cols_dev = trailing.shape[2]
    column_ids = lax.axis_index("row") * cols_dev + jnp.arange(cols_dev, dtype=jnp.int32)
    update = jnp.where(
        column_ids[None, :] < front_order[0], trailing[0] - product, jnp.float32(0.0)
    )
    block_rows = device_rows // BS
    block_cols = cols_dev // BS
    nblocks = block_rows * block_cols
    groups = lax.axis_size("cube")
    own_group = lax.axis_index("cube")
    dest_all = dest_group[:, 0, 0, :, 0]
    parent_all = parent_block[:, 0, 0, :, 0]
    dest_mine = lax.dynamic_index_in_dim(dest_all, own_group, 0, keepdims=False)
    capacity = 2 * nblocks // groups
    nslots = groups * capacity
    hit_table = (dest_mine[:, None] == jnp.arange(groups, dtype=jnp.int32)[None, :]).astype(
        jnp.int32
    )
    before = jnp.cumsum(hit_table, axis=0) - hit_table
    slot_ids = jnp.sum(before * hit_table, axis=1)
    position = dest_mine * capacity + slot_ids
    source_of_slot = (
        jnp.full((nslots,), -1, jnp.int32)
        .at[position]
        .set(jnp.arange(nblocks, dtype=jnp.int32), mode="drop")
    )
    outgoing = pack_blocks(source_of_slot, update, block_cols)
    incoming = lax.all_to_all(
        outgoing.reshape(groups, capacity * BS, BS), "cube", split_axis=0, concat_axis=0, tiled=True
    )
    arriving = dest_all == own_group
    arriving_i = arriving.astype(jnp.int32)
    rank_ids = jnp.cumsum(arriving_i, axis=1) - arriving_i
    in_position = jnp.where(
        arriving,
        jnp.arange(groups, dtype=jnp.int32)[:, None] * capacity + rank_ids,
        nslots,
    )
    parent_of_slot = (
        jnp.full((nslots,), -1, jnp.int32)
        .at[in_position.reshape(-1)]
        .set(parent_all.reshape(-1), mode="drop")
    )
    assembled = combine_blocks(parent_of_slot, incoming.reshape(nslots, BS, BS), parent_front[0])
    return assembled[None]


def pack_kernel(block_cols, source_ref, update_ref, out_ref, sems):
    nslots = out_ref.shape[0]

    def start(slot, carry):
        block = source_ref[slot]

        @pl.when(block >= 0)
        def _():
            rows = pl.ds(pl.multiple_of((block // block_cols) * BS, BS), BS)
            cols = pl.ds(pl.multiple_of((block % block_cols) * BS, BS), BS)
            pltpu.make_async_copy(update_ref.at[rows, cols], out_ref.at[slot], sems.at[slot]).start()

        return carry

    def finish(slot, carry):
        block = source_ref[slot]

        @pl.when(block >= 0)
        def _():
            pltpu.make_async_copy(
                update_ref.at[pl.ds(0, BS), pl.ds(0, BS)], out_ref.at[slot], sems.at[slot]
            ).wait()

        return carry

    lax.fori_loop(0, nslots, start, 0)
    lax.fori_loop(0, nslots, finish, 0)


def pack_blocks(source_of_slot, update, block_cols):
    nslots = source_of_slot.shape[0]
    return pl.pallas_call(
        functools.partial(pack_kernel, block_cols),
        out_shape=jax.ShapeDtypeStruct((nslots, BS, BS), update.dtype),
        in_specs=[
            pl.BlockSpec(memory_space=pltpu.SMEM),
            pl.BlockSpec(memory_space=pltpu.VMEM),
        ],
        out_specs=pl.BlockSpec(memory_space=pl.ANY),
        scratch_shapes=[pltpu.SemaphoreType.DMA((nslots,))],
    )(source_of_slot, update)


def combine_kernel(parent_ref, incoming_ref, front_ref, out_ref):
    out_ref[...] = front_ref[...]

    def body(slot, carry):
        parent = parent_ref[slot]

        @pl.when(parent >= 0)
        def _():
            cols = pl.ds(pl.multiple_of(parent * BS, BS), BS)
            out_ref[:, cols] = out_ref[:, cols] + incoming_ref[slot]

        return carry

    lax.fori_loop(0, incoming_ref.shape[0], body, 0)


def combine_blocks(parent_of_slot, incoming, front):
    return pl.pallas_call(
        combine_kernel,
        out_shape=jax.ShapeDtypeStruct(front.shape, front.dtype),
        in_specs=[
            pl.BlockSpec(memory_space=pltpu.SMEM),
            pl.BlockSpec(memory_space=pltpu.VMEM),
            pl.BlockSpec(memory_space=pltpu.VMEM),
        ],
        out_specs=pl.BlockSpec(memory_space=pltpu.VMEM),
    )(parent_of_slot, incoming, front)


def factor_kernel(a_ref, inv_ref, work_ref, g_ref):
    n = a_ref.shape[0]
    nb = n // BS
    hp = lax.Precision.HIGHEST
    nt = (((1,), (1,)), ((), ()))
    work_ref[...] = a_ref[...]
    lane = lax.broadcasted_iota(jnp.int32, (1, 2 * BS), 1)
    sub = lax.broadcasted_iota(jnp.int32, (BS, BS), 0)
    col = lax.broadcasted_iota(jnp.int32, (BS, BS), 1)
    eye = (sub == col).astype(jnp.float32)
    diag_inv = []
    rid = lax.broadcasted_iota(jnp.int32, (STRIP, 1), 0)
    for k in range(nb):
        kk = pl.ds(k * BS, BS)
        g_ref[:, :BS] = work_ref[kk, kk]
        g_ref[:, BS:] = eye

        for strip in range(0, BS, STRIP):
            held = g_ref[strip:strip + STRIP, :]
            for local in range(STRIP):
                j = strip + local
                row = held[local:local + 1, :]
                factor = jnp.where(rid > local, held[:, j:j + 1] / row[:, j:j + 1], 0.0)
                held = held - factor * row
            pivots = jnp.sum(
                jnp.where(lane[:, :BS] == strip + rid, held[:, :BS], 0.0), axis=1, keepdims=True
            )
            held = held * (1.0 / jnp.sqrt(pivots))
            g_ref[strip:strip + STRIP, :] = held
            below = strip + STRIP
            if below < BS:
                done = g_ref[strip:below, :]
                mult = jnp.transpose(done[:, :BS])[below:, :]
                g_ref[below:, :] = g_ref[below:, :] - jnp.dot(
                    mult, done, precision=hp, preferred_element_type=jnp.float32
                )
        upper = jnp.where(col >= sub, g_ref[:, :BS], 0.0)
        lk_inv = g_ref[:, BS:]
        diag_inv.append(lk_inv)
        work_ref[kk, kk] = jnp.transpose(upper)
        if k < nb - 1:
            rest = pl.ds((k + 1) * BS, n - (k + 1) * BS)
            panel = lax.dot_general(work_ref[rest, kk], lk_inv, nt, precision=hp,
                                    preferred_element_type=jnp.float32)
            work_ref[rest, kk] = panel
            work_ref[rest, rest] = work_ref[rest, rest] - lax.dot_general(
                panel, panel, nt, precision=hp, preferred_element_type=jnp.float32)
    inv_ref[...] = jnp.zeros_like(inv_ref)
    inv_ref[pl.ds(0, BS), pl.ds(0, BS)] = diag_inv[0]
    for i in range(1, nb):
        ii = pl.ds(i * BS, BS)
        left = pl.ds(0, i * BS)
        mixed = jnp.dot(work_ref[ii, left], inv_ref[left, left], precision=hp,
                        preferred_element_type=jnp.float32)
        inv_ref[ii, left] = -jnp.dot(diag_inv[i], mixed, precision=hp,
                                     preferred_element_type=jnp.float32)
        inv_ref[ii, ii] = diag_inv[i]


def factor_inverse(a):
    n = a.shape[0]
    return pl.pallas_call(
        factor_kernel,
        out_shape=jax.ShapeDtypeStruct((n, n), a.dtype),
        in_specs=[pl.BlockSpec(memory_space=pltpu.VMEM)],
        out_specs=pl.BlockSpec(memory_space=pltpu.VMEM),
        scratch_shapes=[pltpu.VMEM((n, n), jnp.float32), pltpu.VMEM((BS, 2 * BS), jnp.float32)],
    )(a)

def solution(mesh):
    placed = (
        P("cube", None, None),
        P("cube", ("row", "col"), None),
        P("cube", "col", "row"),
        P("cube", "col", "row"),
        P("cube"),
        P(None, "col", "row", None, None),
        P(None, "col", "row", None, None),
    )
    return jax.shard_map(
        shards, mesh=mesh, in_specs=placed, out_specs=P("cube", "col", "row"), check_vma=False
    )
```

```python
import functools

import jax
import jax.numpy as jnp
from jax import lax
from jax.experimental import pallas as pl
from jax.experimental.pallas import tpu as pltpu
from jax.sharding import PartitionSpec as P

BS = 128
STRIP = 32


def spread(value, axis, root):
    mine = lax.axis_index(axis) == root
    return lax.psum(jnp.where(mine, value, jnp.zeros_like(value)), axis)


def shards(diag_block, panel, trailing, parent_front, front_order, dest_group, parent_block):
    precise_mode = lax.Precision.HIGHEST
    slab_rows = spread(panel[0], "row", 0)
    col_rows = lax.all_gather(panel[0], "col", axis=0, tiled=True)
    chol_inv = factor_inverse(diag_block[0])
    contract_t = (((1,), (1,)), ((), ()))
    split_mode = lax.Precision.HIGH
    slab_factor = lax.dot_general(slab_rows, chol_inv, contract_t, precision=split_mode)
    slab_solved = jnp.dot(slab_factor, chol_inv, precision=split_mode)
    product = lax.dot_general(slab_solved, col_rows, contract_t, precision=split_mode)
    device_rows = trailing.shape[1]
    cols_dev = trailing.shape[2]
    column_ids = lax.axis_index("row") * cols_dev + jnp.arange(cols_dev, dtype=jnp.int32)
    update = jnp.where(
        column_ids[None, :] < front_order[0], trailing[0] - product, jnp.float32(0.0)
    )
    block_rows = device_rows // BS
    block_cols = cols_dev // BS
    nblocks = block_rows * block_cols
    groups = lax.axis_size("cube")
    own_group = lax.axis_index("cube")
    dest_all = dest_group[:, 0, 0, :, 0]
    parent_all = parent_block[:, 0, 0, :, 0]
    dest_mine = lax.dynamic_index_in_dim(dest_all, own_group, 0, keepdims=False)
    capacity = 2 * nblocks // groups
    nslots = groups * capacity
    hit_table = (dest_mine[:, None] == jnp.arange(groups, dtype=jnp.int32)[None, :]).astype(
        jnp.int32
    )
    before = jnp.cumsum(hit_table, axis=0) - hit_table
    slot_ids = jnp.sum(before * hit_table, axis=1)
    position = dest_mine * capacity + slot_ids
    source_of_slot = (
        jnp.full((nslots,), -1, jnp.int32)
        .at[position]
        .set(jnp.arange(nblocks, dtype=jnp.int32), mode="drop")
    )
    outgoing = pack_blocks(source_of_slot, update, block_cols)
    incoming = lax.all_to_all(
        outgoing.reshape(groups, capacity * BS, BS), "cube", split_axis=0, concat_axis=0, tiled=True
    )
    arriving = dest_all == own_group
    arriving_i = arriving.astype(jnp.int32)
    rank_ids = jnp.cumsum(arriving_i, axis=1) - arriving_i
    in_position = jnp.where(
        arriving,
        jnp.arange(groups, dtype=jnp.int32)[:, None] * capacity + rank_ids,
        nslots,
    )
    parent_of_slot = (
        jnp.full((nslots,), -1, jnp.int32)
        .at[in_position.reshape(-1)]
        .set(parent_all.reshape(-1), mode="drop")
    )
    assembled = combine_blocks(parent_of_slot, incoming.reshape(nslots, BS, BS), parent_front[0])
    return assembled[None]


def pack_kernel(block_cols, source_ref, update_ref, out_ref, sems):
    nslots = out_ref.shape[0]

    def start(slot, carry):
        block = source_ref[slot]

        @pl.when(block >= 0)
        def _():
            rows = pl.ds(pl.multiple_of((block // block_cols) * BS, BS), BS)
            cols = pl.ds(pl.multiple_of((block % block_cols) * BS, BS), BS)
            pltpu.make_async_copy(update_ref.at[rows, cols], out_ref.at[slot], sems.at[slot]).start()

        return carry

    def finish(slot, carry):
        block = source_ref[slot]

        @pl.when(block >= 0)
        def _():
            pltpu.make_async_copy(
                update_ref.at[pl.ds(0, BS), pl.ds(0, BS)], out_ref.at[slot], sems.at[slot]
            ).wait()

        return carry

    lax.fori_loop(0, nslots, start, 0, unroll=8)
    lax.fori_loop(0, nslots, finish, 0, unroll=8)


def pack_blocks(source_of_slot, update, block_cols):
    nslots = source_of_slot.shape[0]
    return pl.pallas_call(
        functools.partial(pack_kernel, block_cols),
        out_shape=jax.ShapeDtypeStruct((nslots, BS, BS), update.dtype),
        in_specs=[
            pl.BlockSpec(memory_space=pltpu.SMEM),
            pl.BlockSpec(memory_space=pltpu.VMEM),
        ],
        out_specs=pl.BlockSpec(memory_space=pl.ANY),
        scratch_shapes=[pltpu.SemaphoreType.DMA((nslots,))],
    )(source_of_slot, update)


def combine_kernel(parent_ref, incoming_ref, front_ref, out_ref):
    out_ref[...] = front_ref[...]

    def body(slot, carry):
        parent = parent_ref[slot]

        @pl.when(parent >= 0)
        def _():
            cols = pl.ds(pl.multiple_of(parent * BS, BS), BS)
            out_ref[:, cols] = out_ref[:, cols] + incoming_ref[slot]

        return carry

    lax.fori_loop(0, incoming_ref.shape[0], body, 0, unroll=8)


def combine_blocks(parent_of_slot, incoming, front):
    return pl.pallas_call(
        combine_kernel,
        out_shape=jax.ShapeDtypeStruct(front.shape, front.dtype),
        in_specs=[
            pl.BlockSpec(memory_space=pltpu.SMEM),
            pl.BlockSpec(memory_space=pltpu.VMEM),
            pl.BlockSpec(memory_space=pltpu.VMEM),
        ],
        out_specs=pl.BlockSpec(memory_space=pltpu.VMEM),
    )(parent_of_slot, incoming, front)


def factor_kernel(a_ref, inv_ref, work_ref, g_ref):
    n = a_ref.shape[0]
    nb = n // BS
    hp = lax.Precision.HIGHEST
    nt = (((1,), (1,)), ((), ()))
    work_ref[...] = a_ref[...]
    lane = lax.broadcasted_iota(jnp.int32, (1, 2 * BS), 1)
    sub = lax.broadcasted_iota(jnp.int32, (BS, BS), 0)
    col = lax.broadcasted_iota(jnp.int32, (BS, BS), 1)
    eye = (sub == col).astype(jnp.float32)
    diag_inv = []
    rid = lax.broadcasted_iota(jnp.int32, (STRIP, 1), 0)
    for k in range(nb):
        kk = pl.ds(k * BS, BS)
        g_ref[:, :BS] = work_ref[kk, kk]
        g_ref[:, BS:] = eye

        for strip in range(0, BS, STRIP):
            held = g_ref[strip:strip + STRIP, :]
            for local in range(STRIP):
                j = strip + local
                row = held[local:local + 1, :]
                factor = jnp.where(rid > local, held[:, j:j + 1] / row[:, j:j + 1], 0.0)
                held = held - factor * row
            pivots = jnp.sum(
                jnp.where(lane[:, :BS] == strip + rid, held[:, :BS], 0.0), axis=1, keepdims=True
            )
            held = held * (1.0 / jnp.sqrt(pivots))
            g_ref[strip:strip + STRIP, :] = held
            below = strip + STRIP
            if below < BS:
                done = g_ref[strip:below, :]
                mult = jnp.transpose(done[:, :BS])[below:, :]
                g_ref[below:, :] = g_ref[below:, :] - jnp.dot(
                    mult, done, precision=hp, preferred_element_type=jnp.float32
                )
        upper = jnp.where(col >= sub, g_ref[:, :BS], 0.0)
        lk_inv = g_ref[:, BS:]
        diag_inv.append(lk_inv)
        work_ref[kk, kk] = jnp.transpose(upper)
        if k < nb - 1:
            rest = pl.ds((k + 1) * BS, n - (k + 1) * BS)
            panel = lax.dot_general(work_ref[rest, kk], lk_inv, nt, precision=hp,
                                    preferred_element_type=jnp.float32)
            work_ref[rest, kk] = panel
            work_ref[rest, rest] = work_ref[rest, rest] - lax.dot_general(
                panel, panel, nt, precision=hp, preferred_element_type=jnp.float32)
    inv_ref[...] = jnp.zeros_like(inv_ref)
    inv_ref[pl.ds(0, BS), pl.ds(0, BS)] = diag_inv[0]
    for i in range(1, nb):
        ii = pl.ds(i * BS, BS)
        left = pl.ds(0, i * BS)
        mixed = jnp.dot(work_ref[ii, left], inv_ref[left, left], precision=hp,
                        preferred_element_type=jnp.float32)
        inv_ref[ii, left] = -jnp.dot(diag_inv[i], mixed, precision=hp,
                                     preferred_element_type=jnp.float32)
        inv_ref[ii, ii] = diag_inv[i]


def factor_inverse(a):
    n = a.shape[0]
    return pl.pallas_call(
        factor_kernel,
        out_shape=jax.ShapeDtypeStruct((n, n), a.dtype),
        in_specs=[pl.BlockSpec(memory_space=pltpu.VMEM)],
        out_specs=pl.BlockSpec(memory_space=pltpu.VMEM),
        scratch_shapes=[pltpu.VMEM((n, n), jnp.float32), pltpu.VMEM((BS, 2 * BS), jnp.float32)],
    )(a)

def solution(mesh):
    placed = (
        P("cube", None, None),
        P("cube", ("row", "col"), None),
        P("cube", "col", "row"),
        P("cube", "col", "row"),
        P("cube"),
        P(None, "col", "row", None, None),
        P(None, "col", "row", None, None),
    )
    return jax.shard_map(
        shards, mesh=mesh, in_specs=placed, out_specs=P("cube", "col", "row"), check_vma=False
    )
```

```python
import functools

import jax
import jax.numpy as jnp
from jax import lax
from jax.experimental import pallas as pl
from jax.experimental.pallas import tpu as pltpu
from jax.sharding import PartitionSpec as P

BS = 128
STRIP = 32


def spread(value, axis, root):
    mine = lax.axis_index(axis) == root
    return lax.psum(jnp.where(mine, value, jnp.zeros_like(value)), axis)


def shards(diag_block, panel, trailing, parent_front, front_order, dest_group, parent_block):
    precise_mode = lax.Precision.HIGHEST
    slab_rows = spread(panel[0], "row", 0)
    col_rows = lax.all_gather(panel[0], "col", axis=0, tiled=True)
    chol_inv = factor_inverse(diag_block[0])
    contract_t = (((1,), (1,)), ((), ()))
    split_mode = lax.Precision.HIGH
    slab_factor = lax.dot_general(slab_rows, chol_inv, contract_t, precision=split_mode)
    slab_solved = jnp.dot(slab_factor, chol_inv, precision=split_mode)
    product = lax.dot_general(slab_solved, col_rows, contract_t, precision=split_mode)
    device_rows = trailing.shape[1]
    cols_dev = trailing.shape[2]
    column_ids = lax.axis_index("row") * cols_dev + jnp.arange(cols_dev, dtype=jnp.int32)
    update = jnp.where(
        column_ids[None, :] < front_order[0], trailing[0] - product, jnp.float32(0.0)
    )
    block_rows = device_rows // BS
    block_cols = cols_dev // BS
    nblocks = block_rows * block_cols
    groups = lax.axis_size("cube")
    own_group = lax.axis_index("cube")
    dest_all = dest_group[:, 0, 0, :, 0]
    parent_all = parent_block[:, 0, 0, :, 0]
    dest_mine = lax.dynamic_index_in_dim(dest_all, own_group, 0, keepdims=False)
    capacity = 2 * nblocks // groups
    nslots = groups * capacity
    hit_table = (dest_mine[:, None] == jnp.arange(groups, dtype=jnp.int32)[None, :]).astype(
        jnp.int32
    )
    before = jnp.cumsum(hit_table, axis=0) - hit_table
    slot_ids = jnp.sum(before * hit_table, axis=1)
    position = dest_mine * capacity + slot_ids
    source_of_slot = (
        jnp.full((nslots,), -1, jnp.int32)
        .at[position]
        .set(jnp.arange(nblocks, dtype=jnp.int32), mode="drop")
    )
    outgoing = pack_blocks(source_of_slot, update, block_cols)
    incoming = lax.all_to_all(
        outgoing.reshape(groups, capacity * BS, BS), "cube", split_axis=0, concat_axis=0, tiled=True
    )
    arriving = dest_all == own_group
    arriving_i = arriving.astype(jnp.int32)
    rank_ids = jnp.cumsum(arriving_i, axis=1) - arriving_i
    in_position = jnp.where(
        arriving,
        jnp.arange(groups, dtype=jnp.int32)[:, None] * capacity + rank_ids,
        nslots,
    )
    parent_of_slot = (
        jnp.full((nslots,), -1, jnp.int32)
        .at[in_position.reshape(-1)]
        .set(parent_all.reshape(-1), mode="drop")
    )
    assembled = combine_blocks(parent_of_slot, incoming.reshape(nslots, BS, BS), parent_front[0])
    return assembled[None]


def pack_kernel(block_cols, source_ref, update_ref, out_ref, sems):
    nslots = out_ref.shape[0]

    def start(slot, carry):
        block = source_ref[slot]

        @pl.when(block >= 0)
        def _():
            rows = pl.ds(pl.multiple_of((block // block_cols) * BS, BS), BS)
            cols = pl.ds(pl.multiple_of((block % block_cols) * BS, BS), BS)
            pltpu.make_async_copy(update_ref.at[rows, cols], out_ref.at[slot], sems.at[slot]).start()

        return carry

    def finish(slot, carry):
        block = source_ref[slot]

        @pl.when(block >= 0)
        def _():
            pltpu.make_async_copy(
                update_ref.at[pl.ds(0, BS), pl.ds(0, BS)], out_ref.at[slot], sems.at[slot]
            ).wait()

        return carry

    lax.fori_loop(0, nslots, start, 0, unroll=True)
    lax.fori_loop(0, nslots, finish, 0, unroll=True)


def pack_blocks(source_of_slot, update, block_cols):
    nslots = source_of_slot.shape[0]
    return pl.pallas_call(
        functools.partial(pack_kernel, block_cols),
        out_shape=jax.ShapeDtypeStruct((nslots, BS, BS), update.dtype),
        in_specs=[
            pl.BlockSpec(memory_space=pltpu.SMEM),
            pl.BlockSpec(memory_space=pltpu.VMEM),
        ],
        out_specs=pl.BlockSpec(memory_space=pl.ANY),
        scratch_shapes=[pltpu.SemaphoreType.DMA((nslots,))],
    )(source_of_slot, update)


def combine_kernel(parent_ref, incoming_ref, front_ref, out_ref):
    out_ref[...] = front_ref[...]

    def body(slot, carry):
        parent = parent_ref[slot]

        @pl.when(parent >= 0)
        def _():
            cols = pl.ds(pl.multiple_of(parent * BS, BS), BS)
            out_ref[:, cols] = out_ref[:, cols] + incoming_ref[slot]

        return carry

    lax.fori_loop(0, incoming_ref.shape[0], body, 0, unroll=True)


def combine_blocks(parent_of_slot, incoming, front):
    return pl.pallas_call(
        combine_kernel,
        out_shape=jax.ShapeDtypeStruct(front.shape, front.dtype),
        in_specs=[
            pl.BlockSpec(memory_space=pltpu.SMEM),
            pl.BlockSpec(memory_space=pltpu.VMEM),
            pl.BlockSpec(memory_space=pltpu.VMEM),
        ],
        out_specs=pl.BlockSpec(memory_space=pltpu.VMEM),
    )(parent_of_slot, incoming, front)


def factor_kernel(a_ref, inv_ref, work_ref, g_ref):
    n = a_ref.shape[0]
    nb = n // BS
    hp = lax.Precision.HIGHEST
    nt = (((1,), (1,)), ((), ()))
    work_ref[...] = a_ref[...]
    lane = lax.broadcasted_iota(jnp.int32, (1, 2 * BS), 1)
    sub = lax.broadcasted_iota(jnp.int32, (BS, BS), 0)
    col = lax.broadcasted_iota(jnp.int32, (BS, BS), 1)
    eye = (sub == col).astype(jnp.float32)
    diag_inv = []
    rid = lax.broadcasted_iota(jnp.int32, (STRIP, 1), 0)
    for k in range(nb):
        kk = pl.ds(k * BS, BS)
        g_ref[:, :BS] = work_ref[kk, kk]
        g_ref[:, BS:] = eye

        for strip in range(0, BS, STRIP):
            held = g_ref[strip:strip + STRIP, :]
            for local in range(STRIP):
                j = strip + local
                row = held[local:local + 1, :]
                factor = jnp.where(rid > local, held[:, j:j + 1] / row[:, j:j + 1], 0.0)
                held = held - factor * row
            pivots = jnp.sum(
                jnp.where(lane[:, :BS] == strip + rid, held[:, :BS], 0.0), axis=1, keepdims=True
            )
            held = held * (1.0 / jnp.sqrt(pivots))
            g_ref[strip:strip + STRIP, :] = held
            below = strip + STRIP
            if below < BS:
                done = g_ref[strip:below, :]
                mult = jnp.transpose(done[:, :BS])[below:, :]
                g_ref[below:, :] = g_ref[below:, :] - jnp.dot(
                    mult, done, precision=hp, preferred_element_type=jnp.float32
                )
        upper = jnp.where(col >= sub, g_ref[:, :BS], 0.0)
        lk_inv = g_ref[:, BS:]
        diag_inv.append(lk_inv)
        work_ref[kk, kk] = jnp.transpose(upper)
        if k < nb - 1:
            rest = pl.ds((k + 1) * BS, n - (k + 1) * BS)
            panel = lax.dot_general(work_ref[rest, kk], lk_inv, nt, precision=hp,
                                    preferred_element_type=jnp.float32)
            work_ref[rest, kk] = panel
            work_ref[rest, rest] = work_ref[rest, rest] - lax.dot_general(
                panel, panel, nt, precision=hp, preferred_element_type=jnp.float32)
    inv_ref[...] = jnp.zeros_like(inv_ref)
    inv_ref[pl.ds(0, BS), pl.ds(0, BS)] = diag_inv[0]
    for i in range(1, nb):
        ii = pl.ds(i * BS, BS)
        left = pl.ds(0, i * BS)
        mixed = jnp.dot(work_ref[ii, left], inv_ref[left, left], precision=hp,
                        preferred_element_type=jnp.float32)
        inv_ref[ii, left] = -jnp.dot(diag_inv[i], mixed, precision=hp,
                                     preferred_element_type=jnp.float32)
        inv_ref[ii, ii] = diag_inv[i]


def factor_inverse(a):
    n = a.shape[0]
    return pl.pallas_call(
        factor_kernel,
        out_shape=jax.ShapeDtypeStruct((n, n), a.dtype),
        in_specs=[pl.BlockSpec(memory_space=pltpu.VMEM)],
        out_specs=pl.BlockSpec(memory_space=pltpu.VMEM),
        scratch_shapes=[pltpu.VMEM((n, n), jnp.float32), pltpu.VMEM((BS, 2 * BS), jnp.float32)],
    )(a)

def solution(mesh):
    placed = (
        P("cube", None, None),
        P("cube", ("row", "col"), None),
        P("cube", "col", "row"),
        P("cube", "col", "row"),
        P("cube"),
        P(None, "col", "row", None, None),
        P(None, "col", "row", None, None),
    )
    return jax.shard_map(
        shards, mesh=mesh, in_specs=placed, out_specs=P("cube", "col", "row"), check_vma=False
    )
```

```python
import functools

import jax
import jax.numpy as jnp
from jax import lax
from jax.experimental import pallas as pl
from jax.experimental.pallas import tpu as pltpu
from jax.sharding import PartitionSpec as P

BS = 128
STRIP = 32


def spread(value, axis, root):
    mine = lax.axis_index(axis) == root
    return lax.psum(jnp.where(mine, value, jnp.zeros_like(value)), axis)


def shards(diag_block, panel, trailing, parent_front, front_order, dest_group, parent_block):
    precise_mode = lax.Precision.HIGHEST
    slab_rows = spread(panel[0], "row", 0)
    col_rows = lax.all_gather(panel[0], "col", axis=0, tiled=True)
    chol_inv = factor_inverse(diag_block[0])
    contract_t = (((1,), (1,)), ((), ()))
    split_mode = lax.Precision.HIGH
    slab_factor = lax.dot_general(slab_rows, chol_inv, contract_t, precision=split_mode)
    slab_solved = jnp.dot(slab_factor, chol_inv, precision=split_mode)
    product = lax.dot_general(slab_solved, col_rows, contract_t, precision=split_mode)
    device_rows = trailing.shape[1]
    cols_dev = trailing.shape[2]
    column_ids = lax.axis_index("row") * cols_dev + jnp.arange(cols_dev, dtype=jnp.int32)
    update = jnp.where(
        column_ids[None, :] < front_order[0], trailing[0] - product, jnp.float32(0.0)
    )
    block_rows = device_rows // BS
    block_cols = cols_dev // BS
    nblocks = block_rows * block_cols
    groups = lax.axis_size("cube")
    own_group = lax.axis_index("cube")
    dest_all = dest_group[:, 0, 0, :, 0]
    parent_all = parent_block[:, 0, 0, :, 0]
    dest_mine = lax.dynamic_index_in_dim(dest_all, own_group, 0, keepdims=False)
    capacity = 2 * nblocks // groups
    nslots = groups * capacity
    hit_table = (dest_mine[:, None] == jnp.arange(groups, dtype=jnp.int32)[None, :]).astype(
        jnp.int32
    )
    before = jnp.cumsum(hit_table, axis=0) - hit_table
    slot_ids = jnp.sum(before * hit_table, axis=1)
    position = dest_mine * capacity + slot_ids
    source_of_slot = (
        jnp.full((nslots,), -1, jnp.int32)
        .at[position]
        .set(jnp.arange(nblocks, dtype=jnp.int32), mode="drop")
    )
    outgoing = pack_blocks(source_of_slot, update, block_cols)
    incoming = lax.all_to_all(
        outgoing.reshape(groups, capacity * BS, BS), "cube", split_axis=0, concat_axis=0, tiled=True
    )
    arriving = dest_all == own_group
    arriving_i = arriving.astype(jnp.int32)
    rank_ids = jnp.cumsum(arriving_i, axis=1) - arriving_i
    in_position = jnp.where(
        arriving,
        jnp.arange(groups, dtype=jnp.int32)[:, None] * capacity + rank_ids,
        nslots,
    )
    parent_of_slot = (
        jnp.full((nslots,), -1, jnp.int32)
        .at[in_position.reshape(-1)]
        .set(parent_all.reshape(-1), mode="drop")
    )
    assembled = combine_blocks(parent_of_slot, incoming.reshape(nslots, BS, BS), parent_front[0])
    return assembled[None]


def pack_kernel(block_cols, source_ref, update_ref, out_ref, sems):
    nslots = out_ref.shape[0]

    def start(slot, carry):
        block = source_ref[slot]

        @pl.when(block >= 0)
        def _():
            rows = pl.ds(pl.multiple_of((block // block_cols) * BS, BS), BS)
            cols = pl.ds(pl.multiple_of((block % block_cols) * BS, BS), BS)
            pltpu.make_async_copy(update_ref.at[rows, cols], out_ref.at[slot], sems.at[slot]).start()

        return carry

    def finish(slot, carry):
        block = source_ref[slot]

        @pl.when(block >= 0)
        def _():
            pltpu.make_async_copy(
                update_ref.at[pl.ds(0, BS), pl.ds(0, BS)], out_ref.at[slot], sems.at[slot]
            ).wait()

        return carry

    lax.fori_loop(0, nslots, start, 0, unroll=8)
    lax.fori_loop(0, nslots, finish, 0, unroll=8)


def pack_blocks(source_of_slot, update, block_cols):
    nslots = source_of_slot.shape[0]
    return pl.pallas_call(
        functools.partial(pack_kernel, block_cols),
        out_shape=jax.ShapeDtypeStruct((nslots, BS, BS), update.dtype),
        in_specs=[
            pl.BlockSpec(memory_space=pltpu.SMEM),
            pl.BlockSpec(memory_space=pltpu.VMEM),
        ],
        out_specs=pl.BlockSpec(memory_space=pl.ANY),
        scratch_shapes=[pltpu.SemaphoreType.DMA((nslots,))],
    )(source_of_slot, update)


def combine_kernel(parent_ref, incoming_ref, front_ref, out_ref):
    out_ref[...] = front_ref[...]

    def body(slot, carry):
        parent = parent_ref[slot]
        cols = pl.ds(pl.multiple_of(jnp.maximum(parent, 0) * BS, BS), BS)
        addend = jnp.where(parent >= 0, incoming_ref[slot], jnp.float32(0.0))
        out_ref[:, cols] = out_ref[:, cols] + addend
        return carry

    lax.fori_loop(0, incoming_ref.shape[0], body, 0, unroll=8)


def combine_blocks(parent_of_slot, incoming, front):
    return pl.pallas_call(
        combine_kernel,
        out_shape=jax.ShapeDtypeStruct(front.shape, front.dtype),
        in_specs=[
            pl.BlockSpec(memory_space=pltpu.SMEM),
            pl.BlockSpec(memory_space=pltpu.VMEM),
            pl.BlockSpec(memory_space=pltpu.VMEM),
        ],
        out_specs=pl.BlockSpec(memory_space=pltpu.VMEM),
    )(parent_of_slot, incoming, front)


def factor_kernel(a_ref, inv_ref, work_ref, g_ref):
    n = a_ref.shape[0]
    nb = n // BS
    hp = lax.Precision.HIGHEST
    nt = (((1,), (1,)), ((), ()))
    work_ref[...] = a_ref[...]
    lane = lax.broadcasted_iota(jnp.int32, (1, 2 * BS), 1)
    sub = lax.broadcasted_iota(jnp.int32, (BS, BS), 0)
    col = lax.broadcasted_iota(jnp.int32, (BS, BS), 1)
    eye = (sub == col).astype(jnp.float32)
    diag_inv = []
    rid = lax.broadcasted_iota(jnp.int32, (STRIP, 1), 0)
    for k in range(nb):
        kk = pl.ds(k * BS, BS)
        g_ref[:, :BS] = work_ref[kk, kk]
        g_ref[:, BS:] = eye

        for strip in range(0, BS, STRIP):
            held = g_ref[strip:strip + STRIP, :]
            for local in range(STRIP):
                j = strip + local
                row = held[local:local + 1, :]
                factor = jnp.where(rid > local, held[:, j:j + 1] / row[:, j:j + 1], 0.0)
                held = held - factor * row
            pivots = jnp.sum(
                jnp.where(lane[:, :BS] == strip + rid, held[:, :BS], 0.0), axis=1, keepdims=True
            )
            held = held * (1.0 / jnp.sqrt(pivots))
            g_ref[strip:strip + STRIP, :] = held
            below = strip + STRIP
            if below < BS:
                done = g_ref[strip:below, :]
                mult = jnp.transpose(done[:, :BS])[below:, :]
                g_ref[below:, :] = g_ref[below:, :] - jnp.dot(
                    mult, done, precision=hp, preferred_element_type=jnp.float32
                )
        upper = jnp.where(col >= sub, g_ref[:, :BS], 0.0)
        lk_inv = g_ref[:, BS:]
        diag_inv.append(lk_inv)
        work_ref[kk, kk] = jnp.transpose(upper)
        if k < nb - 1:
            rest = pl.ds((k + 1) * BS, n - (k + 1) * BS)
            panel = lax.dot_general(work_ref[rest, kk], lk_inv, nt, precision=hp,
                                    preferred_element_type=jnp.float32)
            work_ref[rest, kk] = panel
            work_ref[rest, rest] = work_ref[rest, rest] - lax.dot_general(
                panel, panel, nt, precision=hp, preferred_element_type=jnp.float32)
    inv_ref[...] = jnp.zeros_like(inv_ref)
    inv_ref[pl.ds(0, BS), pl.ds(0, BS)] = diag_inv[0]
    for i in range(1, nb):
        ii = pl.ds(i * BS, BS)
        left = pl.ds(0, i * BS)
        mixed = jnp.dot(work_ref[ii, left], inv_ref[left, left], precision=hp,
                        preferred_element_type=jnp.float32)
        inv_ref[ii, left] = -jnp.dot(diag_inv[i], mixed, precision=hp,
                                     preferred_element_type=jnp.float32)
        inv_ref[ii, ii] = diag_inv[i]


def factor_inverse(a):
    n = a.shape[0]
    return pl.pallas_call(
        factor_kernel,
        out_shape=jax.ShapeDtypeStruct((n, n), a.dtype),
        in_specs=[pl.BlockSpec(memory_space=pltpu.VMEM)],
        out_specs=pl.BlockSpec(memory_space=pltpu.VMEM),
        scratch_shapes=[pltpu.VMEM((n, n), jnp.float32), pltpu.VMEM((BS, 2 * BS), jnp.float32)],
    )(a)

def solution(mesh):
    placed = (
        P("cube", None, None),
        P("cube", ("row", "col"), None),
        P("cube", "col", "row"),
        P("cube", "col", "row"),
        P("cube"),
        P(None, "col", "row", None, None),
        P(None, "col", "row", None, None),
    )
    return jax.shard_map(
        shards, mesh=mesh, in_specs=placed, out_specs=P("cube", "col", "row"), check_vma=False
    )
```

```python
import functools

import jax
import jax.numpy as jnp
from jax import lax
from jax.experimental import pallas as pl
from jax.experimental.pallas import tpu as pltpu
from jax.sharding import PartitionSpec as P

BS = 128
STRIP = 32


def spread(value, axis, root):
    mine = lax.axis_index(axis) == root
    return lax.psum(jnp.where(mine, value, jnp.zeros_like(value)), axis)


def shards(diag_block, panel, trailing, parent_front, front_order, dest_group, parent_block):
    precise_mode = lax.Precision.HIGHEST
    slab_rows = spread(panel[0], "row", 0)
    col_rows = lax.all_gather(panel[0], "col", axis=0, tiled=True)
    chol_inv = factor_inverse(diag_block[0])
    contract_t = (((1,), (1,)), ((), ()))
    split_mode = lax.Precision.HIGH
    slab_factor = lax.dot_general(slab_rows, chol_inv, contract_t, precision=split_mode)
    slab_solved = jnp.dot(slab_factor, chol_inv, precision=split_mode)
    product = lax.dot_general(slab_solved, col_rows, contract_t, precision=split_mode)
    device_rows = trailing.shape[1]
    cols_dev = trailing.shape[2]
    column_ids = lax.axis_index("row") * cols_dev + jnp.arange(cols_dev, dtype=jnp.int32)
    update = jnp.where(
        column_ids[None, :] < front_order[0], trailing[0] - product, jnp.float32(0.0)
    )
    block_rows = device_rows // BS
    block_cols = cols_dev // BS
    nblocks = block_rows * block_cols
    groups = lax.axis_size("cube")
    own_group = lax.axis_index("cube")
    dest_all = dest_group[:, 0, 0, :, 0]
    parent_all = parent_block[:, 0, 0, :, 0]
    dest_mine = lax.dynamic_index_in_dim(dest_all, own_group, 0, keepdims=False)
    capacity = 2 * nblocks // groups
    nslots = groups * capacity
    hit_table = (dest_mine[:, None] == jnp.arange(groups, dtype=jnp.int32)[None, :]).astype(
        jnp.int32
    )
    before = jnp.cumsum(hit_table, axis=0) - hit_table
    slot_ids = jnp.sum(before * hit_table, axis=1)
    position = dest_mine * capacity + slot_ids
    source_of_slot = (
        jnp.full((nslots,), -1, jnp.int32)
        .at[position]
        .set(jnp.arange(nblocks, dtype=jnp.int32), mode="drop")
    )
    outgoing = pack_blocks(source_of_slot, update, block_cols)
    incoming = lax.all_to_all(
        outgoing.reshape(groups, capacity * BS, BS), "cube", split_axis=0, concat_axis=0, tiled=True
    )
    arriving = dest_all == own_group
    arriving_i = arriving.astype(jnp.int32)
    rank_ids = jnp.cumsum(arriving_i, axis=1) - arriving_i
    in_position = jnp.where(
        arriving,
        jnp.arange(groups, dtype=jnp.int32)[:, None] * capacity + rank_ids,
        nslots,
    )
    parent_of_slot = (
        jnp.full((nslots,), -1, jnp.int32)
        .at[in_position.reshape(-1)]
        .set(parent_all.reshape(-1), mode="drop")
    )
    assembled = combine_blocks(parent_of_slot, incoming.reshape(nslots, BS, BS), parent_front[0])
    return assembled[None]


def pack_kernel(block_cols, source_ref, update_ref, out_ref, sems):
    nslots = out_ref.shape[0]

    def start(slot, carry):
        block = source_ref[slot]

        @pl.when(block >= 0)
        def _():
            rows = pl.ds(pl.multiple_of((block // block_cols) * BS, BS), BS)
            cols = pl.ds(pl.multiple_of((block % block_cols) * BS, BS), BS)
            pltpu.make_async_copy(update_ref.at[rows, cols], out_ref.at[slot], sems.at[slot]).start()

        return carry

    def finish(slot, carry):
        block = source_ref[slot]

        @pl.when(block >= 0)
        def _():
            pltpu.make_async_copy(
                update_ref.at[pl.ds(0, BS), pl.ds(0, BS)], out_ref.at[slot], sems.at[slot]
            ).wait()

        return carry

    lax.fori_loop(0, nslots, start, 0, unroll=8)
    lax.fori_loop(0, nslots, finish, 0, unroll=8)


def pack_blocks(source_of_slot, update, block_cols):
    nslots = source_of_slot.shape[0]
    return pl.pallas_call(
        functools.partial(pack_kernel, block_cols),
        out_shape=jax.ShapeDtypeStruct((nslots, BS, BS), update.dtype),
        in_specs=[
            pl.BlockSpec(memory_space=pltpu.SMEM),
            pl.BlockSpec(memory_space=pltpu.VMEM),
        ],
        out_specs=pl.BlockSpec(memory_space=pl.ANY),
        scratch_shapes=[pltpu.SemaphoreType.DMA((nslots,))],
    )(source_of_slot, update)


def combine_kernel(parent_ref, incoming_ref, front_ref, out_ref):
    out_ref[...] = front_ref[...]

    def body(slot, carry):
        parent = parent_ref[slot]

        @pl.when(parent >= 0)
        def _():
            cols = pl.ds(pl.multiple_of(parent * BS, BS), BS)
            out_ref[:, cols] = out_ref[:, cols] + incoming_ref[slot]

        return carry

    lax.fori_loop(0, incoming_ref.shape[0], body, 0, unroll=8)


def combine_blocks(parent_of_slot, incoming, front):
    return pl.pallas_call(
        combine_kernel,
        out_shape=jax.ShapeDtypeStruct(front.shape, front.dtype),
        in_specs=[
            pl.BlockSpec(memory_space=pltpu.SMEM),
            pl.BlockSpec(memory_space=pltpu.VMEM),
            pl.BlockSpec(memory_space=pltpu.VMEM),
        ],
        out_specs=pl.BlockSpec(memory_space=pltpu.VMEM),
    )(parent_of_slot, incoming, front)


def factor_kernel(a_ref, inv_ref, work_ref, g_ref):
    n = a_ref.shape[0]
    nb = n // BS
    hp = lax.Precision.HIGHEST
    nt = (((1,), (1,)), ((), ()))
    work_ref[...] = a_ref[...]
    lane = lax.broadcasted_iota(jnp.int32, (1, 2 * BS), 1)
    sub = lax.broadcasted_iota(jnp.int32, (BS, BS), 0)
    col = lax.broadcasted_iota(jnp.int32, (BS, BS), 1)
    eye = (sub == col).astype(jnp.float32)
    diag_inv = []
    rid = lax.broadcasted_iota(jnp.int32, (STRIP, 1), 0)
    for k in range(nb):
        kk = pl.ds(k * BS, BS)
        g_ref[:, :BS] = work_ref[kk, kk]
        g_ref[:, BS:] = eye

        for strip in range(0, BS, STRIP):
            held = g_ref[strip:strip + STRIP, :]
            for local in range(STRIP):
                j = strip + local
                row = held[local:local + 1, :]
                factor = jnp.where(rid > local, held[:, j:j + 1] / row[:, j:j + 1], 0.0)
                held = held - factor * row
            pivots = jnp.sum(
                jnp.where(lane[:, :BS] == strip + rid, held[:, :BS], 0.0), axis=1, keepdims=True
            )
            held = held * (1.0 / jnp.sqrt(pivots))
            g_ref[strip:strip + STRIP, :] = held
            below = strip + STRIP
            if below < BS:
                done = g_ref[strip:below, :]
                mult = jnp.transpose(done[:, :BS])[below:, :]
                g_ref[below:, :] = g_ref[below:, :] - jnp.dot(
                    mult, done, precision=hp, preferred_element_type=jnp.float32
                )
        upper = jnp.where(col >= sub, g_ref[:, :BS], 0.0)
        lk_inv = g_ref[:, BS:]
        diag_inv.append(lk_inv)
        work_ref[kk, kk] = jnp.transpose(upper)
        if k < nb - 1:
            rest = pl.ds((k + 1) * BS, n - (k + 1) * BS)
            panel = lax.dot_general(work_ref[rest, kk], lk_inv, nt, precision=hp,
                                    preferred_element_type=jnp.float32)
            work_ref[rest, kk] = panel
            work_ref[rest, rest] = work_ref[rest, rest] - lax.dot_general(
                panel, panel, nt, precision=hp, preferred_element_type=jnp.float32)
    inv_ref[...] = jnp.zeros_like(inv_ref)
    inv_ref[pl.ds(0, BS), pl.ds(0, BS)] = diag_inv[0]
    for i in range(1, nb):
        ii = pl.ds(i * BS, BS)
        left = pl.ds(0, i * BS)
        mixed = jnp.dot(work_ref[ii, left], inv_ref[left, left], precision=lax.Precision.HIGH,
                        preferred_element_type=jnp.float32)
        inv_ref[ii, left] = -jnp.dot(diag_inv[i], mixed, precision=lax.Precision.HIGH,
                                     preferred_element_type=jnp.float32)
        inv_ref[ii, ii] = diag_inv[i]


def factor_inverse(a):
    n = a.shape[0]
    return pl.pallas_call(
        factor_kernel,
        out_shape=jax.ShapeDtypeStruct((n, n), a.dtype),
        in_specs=[pl.BlockSpec(memory_space=pltpu.VMEM)],
        out_specs=pl.BlockSpec(memory_space=pltpu.VMEM),
        scratch_shapes=[pltpu.VMEM((n, n), jnp.float32), pltpu.VMEM((BS, 2 * BS), jnp.float32)],
    )(a)

def solution(mesh):
    placed = (
        P("cube", None, None),
        P("cube", ("row", "col"), None),
        P("cube", "col", "row"),
        P("cube", "col", "row"),
        P("cube"),
        P(None, "col", "row", None, None),
        P(None, "col", "row", None, None),
    )
    return jax.shard_map(
        shards, mesh=mesh, in_specs=placed, out_specs=P("cube", "col", "row"), check_vma=False
    )
```

```python
import functools

import jax
import jax.numpy as jnp
from jax import lax
from jax.experimental import pallas as pl
from jax.experimental.pallas import tpu as pltpu
from jax.sharding import PartitionSpec as P

BS = 128
STRIP = 32


def spread(value, axis, root):
    mine = lax.axis_index(axis) == root
    return lax.psum(jnp.where(mine, value, jnp.zeros_like(value)), axis)


def shards(diag_block, panel, trailing, parent_front, front_order, dest_group, parent_block):
    precise_mode = lax.Precision.HIGHEST
    slab_rows = spread(panel[0], "row", 0)
    col_rows = lax.all_gather(panel[0], "col", axis=0, tiled=True)
    chol_inv = factor_inverse(diag_block[0])
    contract_t = (((1,), (1,)), ((), ()))
    split_mode = lax.Precision.HIGH
    slab_factor = lax.dot_general(slab_rows, chol_inv, contract_t, precision=split_mode)
    slab_solved = jnp.dot(slab_factor, chol_inv, precision=split_mode)
    product = lax.dot_general(slab_solved, col_rows, contract_t, precision=split_mode)
    device_rows = trailing.shape[1]
    cols_dev = trailing.shape[2]
    column_ids = lax.axis_index("row") * cols_dev + jnp.arange(cols_dev, dtype=jnp.int32)
    update = jnp.where(
        column_ids[None, :] < front_order[0], trailing[0] - product, jnp.float32(0.0)
    )
    block_rows = device_rows // BS
    block_cols = cols_dev // BS
    nblocks = block_rows * block_cols
    groups = lax.axis_size("cube")
    own_group = lax.axis_index("cube")
    dest_all = dest_group[:, 0, 0, :, 0]
    parent_all = parent_block[:, 0, 0, :, 0]
    dest_mine = lax.dynamic_index_in_dim(dest_all, own_group, 0, keepdims=False)
    capacity = 2 * nblocks // groups
    nslots = groups * capacity
    hit_table = (dest_mine[:, None] == jnp.arange(groups, dtype=jnp.int32)[None, :]).astype(
        jnp.int32
    )
    before = jnp.cumsum(hit_table, axis=0) - hit_table
    slot_ids = jnp.sum(before * hit_table, axis=1)
    position = dest_mine * capacity + slot_ids
    source_of_slot = (
        jnp.full((nslots,), -1, jnp.int32)
        .at[position]
        .set(jnp.arange(nblocks, dtype=jnp.int32), mode="drop")
    )
    outgoing = pack_blocks(source_of_slot, update, block_cols)
    incoming = lax.all_to_all(
        outgoing.reshape(groups, capacity * BS, BS), "cube", split_axis=0, concat_axis=0, tiled=True
    )
    arriving = dest_all == own_group
    arriving_i = arriving.astype(jnp.int32)
    rank_ids = jnp.cumsum(arriving_i, axis=1) - arriving_i
    in_position = jnp.where(
        arriving,
        jnp.arange(groups, dtype=jnp.int32)[:, None] * capacity + rank_ids,
        nslots,
    )
    parent_of_slot = (
        jnp.full((nslots,), -1, jnp.int32)
        .at[in_position.reshape(-1)]
        .set(parent_all.reshape(-1), mode="drop")
    )
    assembled = combine_blocks(parent_of_slot, incoming.reshape(nslots, BS, BS), parent_front[0])
    return assembled[None]


def pack_kernel(block_cols, source_ref, update_ref, out_ref, sems):
    nslots = out_ref.shape[0]

    def start(slot, carry):
        block = source_ref[slot]

        @pl.when(block >= 0)
        def _():
            rows = pl.ds(pl.multiple_of((block // block_cols) * BS, BS), BS)
            cols = pl.ds(pl.multiple_of((block % block_cols) * BS, BS), BS)
            pltpu.make_async_copy(update_ref.at[rows, cols], out_ref.at[slot], sems.at[slot]).start()

        return carry

    def finish(slot, carry):
        block = source_ref[slot]

        @pl.when(block >= 0)
        def _():
            pltpu.make_async_copy(
                update_ref.at[pl.ds(0, BS), pl.ds(0, BS)], out_ref.at[slot], sems.at[slot]
            ).wait()

        return carry

    lax.fori_loop(0, nslots, start, 0, unroll=8)
    lax.fori_loop(0, nslots, finish, 0, unroll=8)


def pack_blocks(source_of_slot, update, block_cols):
    nslots = source_of_slot.shape[0]
    return pl.pallas_call(
        functools.partial(pack_kernel, block_cols),
        out_shape=jax.ShapeDtypeStruct((nslots, BS, BS), update.dtype),
        in_specs=[
            pl.BlockSpec(memory_space=pltpu.SMEM),
            pl.BlockSpec(memory_space=pltpu.VMEM),
        ],
        out_specs=pl.BlockSpec(memory_space=pl.ANY),
        scratch_shapes=[pltpu.SemaphoreType.DMA((nslots,))],
    )(source_of_slot, update)


def combine_kernel(parent_ref, incoming_ref, front_ref, out_ref):
    out_ref[...] = front_ref[...]

    def body(slot, carry):
        parent = parent_ref[slot]

        @pl.when(parent >= 0)
        def _():
            cols = pl.ds(pl.multiple_of(parent * BS, BS), BS)
            out_ref[:, cols] = out_ref[:, cols] + incoming_ref[slot]

        return carry

    lax.fori_loop(0, incoming_ref.shape[0], body, 0, unroll=8)


def combine_blocks(parent_of_slot, incoming, front):
    return pl.pallas_call(
        combine_kernel,
        out_shape=jax.ShapeDtypeStruct(front.shape, front.dtype),
        in_specs=[
            pl.BlockSpec(memory_space=pltpu.SMEM),
            pl.BlockSpec(memory_space=pltpu.VMEM),
            pl.BlockSpec(memory_space=pltpu.VMEM),
        ],
        out_specs=pl.BlockSpec(memory_space=pltpu.VMEM),
    )(parent_of_slot, incoming, front)


def factor_kernel(a_ref, inv_ref, work_ref, g_ref, load_sem):
    n = a_ref.shape[0]
    nb = n // BS
    hp = lax.Precision.HIGHEST
    nt = (((1,), (1,)), ((), ()))
    load = pltpu.make_async_copy(a_ref, work_ref, load_sem)
    load.start()
    load.wait()
    lane = lax.broadcasted_iota(jnp.int32, (1, 2 * BS), 1)
    sub = lax.broadcasted_iota(jnp.int32, (BS, BS), 0)
    col = lax.broadcasted_iota(jnp.int32, (BS, BS), 1)
    eye = (sub == col).astype(jnp.float32)
    diag_inv = []
    rid = lax.broadcasted_iota(jnp.int32, (STRIP, 1), 0)
    for k in range(nb):
        kk = pl.ds(k * BS, BS)
        g_ref[:, :BS] = work_ref[kk, kk]
        g_ref[:, BS:] = eye

        for strip in range(0, BS, STRIP):
            held = g_ref[strip:strip + STRIP, :]
            for local in range(STRIP):
                j = strip + local
                row = held[local:local + 1, :]
                factor = jnp.where(rid > local, held[:, j:j + 1] / row[:, j:j + 1], 0.0)
                held = held - factor * row
            pivots = jnp.sum(
                jnp.where(lane[:, :BS] == strip + rid, held[:, :BS], 0.0), axis=1, keepdims=True
            )
            held = held * (1.0 / jnp.sqrt(pivots))
            g_ref[strip:strip + STRIP, :] = held
            below = strip + STRIP
            if below < BS:
                done = g_ref[strip:below, :]
                mult = jnp.transpose(done[:, :BS])[below:, :]
                g_ref[below:, :] = g_ref[below:, :] - jnp.dot(
                    mult, done, precision=hp, preferred_element_type=jnp.float32
                )
        upper = jnp.where(col >= sub, g_ref[:, :BS], 0.0)
        lk_inv = g_ref[:, BS:]
        diag_inv.append(lk_inv)
        work_ref[kk, kk] = jnp.transpose(upper)
        if k < nb - 1:
            rest = pl.ds((k + 1) * BS, n - (k + 1) * BS)
            panel = lax.dot_general(work_ref[rest, kk], lk_inv, nt, precision=hp,
                                    preferred_element_type=jnp.float32)
            work_ref[rest, kk] = panel
            work_ref[rest, rest] = work_ref[rest, rest] - lax.dot_general(
                panel, panel, nt, precision=hp, preferred_element_type=jnp.float32)
    inv_ref[...] = jnp.zeros_like(inv_ref)
    inv_ref[pl.ds(0, BS), pl.ds(0, BS)] = diag_inv[0]
    for i in range(1, nb):
        ii = pl.ds(i * BS, BS)
        left = pl.ds(0, i * BS)
        mixed = jnp.dot(work_ref[ii, left], inv_ref[left, left], precision=hp,
                        preferred_element_type=jnp.float32)
        inv_ref[ii, left] = -jnp.dot(diag_inv[i], mixed, precision=hp,
                                     preferred_element_type=jnp.float32)
        inv_ref[ii, ii] = diag_inv[i]


def factor_inverse(a):
    n = a.shape[0]
    return pl.pallas_call(
        factor_kernel,
        out_shape=jax.ShapeDtypeStruct((n, n), a.dtype),
        in_specs=[pl.BlockSpec(memory_space=pl.ANY)],
        out_specs=pl.BlockSpec(memory_space=pltpu.VMEM),
        scratch_shapes=[
            pltpu.VMEM((n, n), jnp.float32),
            pltpu.VMEM((BS, 2 * BS), jnp.float32),
            pltpu.SemaphoreType.DMA(()),
        ],
    )(a)

def solution(mesh):
    placed = (
        P("cube", None, None),
        P("cube", ("row", "col"), None),
        P("cube", "col", "row"),
        P("cube", "col", "row"),
        P("cube"),
        P(None, "col", "row", None, None),
        P(None, "col", "row", None, None),
    )
    return jax.shard_map(
        shards, mesh=mesh, in_specs=placed, out_specs=P("cube", "col", "row"), check_vma=False
    )
```
